32 devices in a mesh: dp: 8 (over y, x, core), group: 4 (over z).
Axes of the slice: x: 2, y: 2, z: 4, core: 2. Of those that a mesh axis runs over, the one named last changes fastest.
Arguments:
- images: bfloat16 [64, 196, 512], P(('dp', 'group')), may hold values from -6 to 6
- grad_output: bfloat16 [64, 196, 512], P(('dp', 'group')), may hold values from -6 to 6
- live_count: int32 [8, 4], P('dp', 'group'), may hold values from 1 to 2, as said below
- qkv_weight: float32 [512, 1536], P(None, 'group'), may hold values from -0.25 to 0.25
- proj_weight: float32 [512, 512], P(None, 'group'), may hold values from -0.75 to 0.75
- up_weight: float32 [512, 2048], P(None, 'group'), may hold values from -0.25 to 0.25
- down_weight: float32 [2048, 512], P('group'), may hold values from -0.125 to 0.125
- qkv_moment: float32 [512, 1536], P(None, 'group'), may hold values from -360 to 360
- proj_moment: float32 [512, 512], P(None, 'group'), may hold values from -360 to 360
- up_moment: float32 [512, 2048], P(None, 'group'), may hold values from -360 to 360
- down_moment: float32 [2048, 512], P('group'), may hold values from -360 to 360
- vectors: float32 [8, 512], replicated
- hidden_bias: float32 [2048], replicated, may hold values from -2 to 2
- rel_table: float32 [169, 16], replicated, may hold values from -4 to 4
- vector_first: float32 [8, 512], replicated, may hold values from -30 to 30
- vector_second: float32 [8, 512], replicated, may hold values from 1 to 30
- bias_first: float32 [2048], replicated, may hold values from -30 to 30
- bias_second: float32 [2048], replicated, may hold values from 1 to 30
- table_first: float32 [169, 16], replicated, may hold values from -30 to 30
- table_second: float32 [169, 16], replicated, may hold values from 1 to 30
Outputs:
- output: bfloat16 [64, 196, 512], P(('dp', 'group'))
- input_grad: float32 [64, 196, 512], P(('dp', 'group'))
- qkv_grad: float32 [512, 1536], P(None, 'group')
- proj_grad: float32 [512, 512], P(None, 'group')
- up_grad: float32 [512, 2048], P(None, 'group')
- down_grad: float32 [2048, 512], P('group')
- vector_grad: float32 [8, 512], replicated
- bias_grad: float32 [2048], replicated
- table_grad: float32 [169, 16], replicated
- new_qkv: float32 [512, 1536], P(None, 'group')
- new_proj: float32 [512, 512], P(None, 'group')
- new_up: float32 [512, 2048], P(None, 'group')
- new_down: float32 [2048, 512], P('group')
- qkv_momentum: float32 [512, 1536], P(None, 'group')
- proj_momentum: float32 [512, 512], P(None, 'group')
- up_momentum: float32 [512, 2048], P(None, 'group')
- down_momentum: float32 [2048, 512], P('group')
- new_vectors: float32 [8, 512], replicated
- new_bias: float32 [2048], replicated
- new_table: float32 [169, 16], replicated
- vector_mean: float32 [8, 512], replicated
- vector_square: float32 [8, 512], replicated
- bias_mean: float32 [2048], replicated
- bias_square: float32 [2048], replicated
- table_mean: float32 [169, 16], replicated
- table_square: float32 [169, 16], replicated
The draws below stay inside these ranges and needn't reach their ends.
Inputs may be any that keep to these rules, and one draw needn't show every extreme that they name: Each device holds live images in its first live_count slots; every device has at least one, and some device is full in every draw.
All inputs are finite; a program needn't handle non-finite values.
Results may differ from the reference program's by a relative error of at most 0.017.
Values may be sent and summed in bfloat16 or wider, within the bound.
No kernel may reach another device: no remote copies, remote signals or barrier semaphores. Data moves between devices by JAX's collectives and lax.ppermute only.
A program may use at most 128 MiB of HBM per device.

```python
import math
import jax
import jax.numpy as jnp
import numpy as np
from jax import lax

D = 512
HEADS = 16
FF = 2048
SIDE = 14
WIN = 7
SHIFT = 3
NS_STEPS = 5
SLOTS = 2
IMAGES = 64
REL = 169
N_DP = 8
N_GROUP = 4


def draw_live_count(key, part):
    first_key = jax.random.fold_in(key, 11)
    second_key = jax.random.fold_in(key, 12)
    third_key = jax.random.fold_in(key, 13)
    device_total = N_DP * N_GROUP
    base = jax.random.randint(first_key, (device_total,), 1, SLOTS // 2 + 1)
    heavy = jax.random.randint(second_key, (device_total,), 0, 8) == 0
    counts = jnp.where(heavy, SLOTS, base)
    chosen = jax.random.randint(third_key, (), 0, device_total)
    counts = jnp.where(jnp.arange(device_total) == chosen, SLOTS, counts)
    return counts.reshape(N_DP, N_GROUP).astype(jnp.int32)


def draw_vectors(key, part):
    noise = jax.random.normal(jax.random.fold_in(key, 21), (8, D), jnp.float32)
    rows_index = jnp.arange(8)
    gains = (rows_index == 0) | (rows_index == 5)
    return jnp.where(gains[:, None], 1.0 + 0.15 * noise, 0.3 * noise).astype(jnp.float32)


def steps_of(key, shape, shards, least, top_value):
    loudness, own = 1.0, jax.random.fold_in(key, 6)
    for axis_at, parts in shards:
        heights = jnp.exp(jax.random.uniform(jax.random.fold_in(own, axis_at), (parts,), jnp.float32, least / len(shards), top_value / len(shards)))
        loudness = loudness * jnp.repeat(heights, shape[axis_at] // parts).reshape([-1 if axis == axis_at else 1 for axis in range(len(shape))])
    return loudness


def normal_values(own_key, shape, spread, reach, shards=(), kind=jnp.bfloat16):
    level = steps_of(own_key, shape, shards, -0.22, 0.18) if shards else 1.0
    values = jax.random.normal(own_key, shape, jnp.float32) * spread * level
    return jnp.minimum(jnp.maximum(values, -reach), reach).astype(kind)


def setup_inputs(seed: int = 0) -> dict:
    key_list = jax.random.split(jax.random.key(seed), 21)
    return {
        "images": normal_values(key_list[0], (IMAGES, SIDE * SIDE, D), 1.0, 6.0, ((0, 32),)),
        "grad_output": normal_values(key_list[1], (IMAGES, SIDE * SIDE, D), 1.0, 6.0, ((0, 32),)),
        "live_count": draw_live_count(jax.random.fold_in(key_list[20], 71), 0),
        "qkv_weight": normal_values(key_list[3], (D, 3 * D), D ** -0.5, 0.25, ((1, 4),), jnp.float32),
        "proj_weight": normal_values(key_list[4], (D, D), (D // 8) ** -0.5, 0.75, ((1, 4),), jnp.float32),
        "up_weight": normal_values(key_list[5], (D, FF), D ** -0.5, 0.25, ((1, 4),), jnp.float32),
        "down_weight": normal_values(key_list[6], (FF, D), FF ** -0.5, 0.125, ((0, 4),), jnp.float32),
        "qkv_moment": normal_values(key_list[7], (D, 3 * D), 60.0, 360.0, ((1, 4),), jnp.float32),
        "proj_moment": normal_values(key_list[8], (D, D), 60.0, 360.0, ((1, 4),), jnp.float32),
        "up_moment": normal_values(key_list[9], (D, FF), 60.0, 360.0, ((1, 4),), jnp.float32),
        "down_moment": normal_values(key_list[10], (FF, D), 60.0, 360.0, ((0, 4),), jnp.float32),
        "vectors": draw_vectors(jax.random.fold_in(key_list[20], 71), 0),
        "hidden_bias": normal_values(key_list[12], (FF,), 0.3, 2.0, (), jnp.float32),
        "rel_table": normal_values(key_list[13], (REL, HEADS), 1.0, 4.0, (), jnp.float32),
        "vector_first": normal_values(key_list[14], (8, D), 5.0, 30.0, (), jnp.float32),
        "vector_second": jnp.clip(jnp.exp(jax.random.uniform(key_list[15], (8, D), jnp.float32, math.log(1.0), math.log(30.0))), 1.0, 30.0),
        "bias_first": normal_values(key_list[16], (FF,), 5.0, 30.0, (), jnp.float32),
        "bias_second": jnp.clip(jnp.exp(jax.random.uniform(key_list[17], (FF,), jnp.float32, math.log(1.0), math.log(30.0))), 1.0, 30.0),
        "table_first": normal_values(key_list[18], (REL, HEADS), 5.0, 30.0, (), jnp.float32),
        "table_second": jnp.clip(jnp.exp(jax.random.uniform(key_list[19], (REL, HEADS), jnp.float32, math.log(1.0), math.log(30.0))), 1.0, 30.0),
    }


norm_eps = 1e-05
mask_fill = -100.0
muon_momentum = 0.95
muon_rate = 0.4
muon_decay = 0.1
adam_rate = 0.1
beta_first = 0.9
beta_second = 0.999
adam_eps = 1e-08
adam_count = 10.0
frob_eps = 1e-06
newton_first = 3.4445
newton_second = -4.775
newton_third = 2.0315

def window_tables(side, window, shift):
    steps = np.arange(window)
    row_pos = np.repeat(steps, window)
    col_pos = np.tile(steps, window)
    span = 2 * window - 1
    offset = (row_pos[:, None] - row_pos[None, :] + window - 1) * span + (col_pos[:, None] - col_pos[None, :] + window - 1)
    onehot = (offset.reshape(-1)[:, None] == np.arange(span * span)[None, :]).astype(np.float32)
    line = np.arange(side)
    label = (line >= side - window).astype(np.int64) + (line >= side - shift).astype(np.int64)
    region = 3 * label[:, None] + label[None, :]
    per_side = side // window
    region = region.reshape(per_side, window, per_side, window).transpose(0, 2, 1, 3).reshape(per_side * per_side, window * window)
    blocked = np.where(region[:, :, None] != region[:, None, :], mask_fill, 0.0).astype(np.float32)
    return (jnp.asarray(onehot), jnp.asarray(blocked))

def to_windows(tensor):
    slot_total, channel = (tensor.shape[0], tensor.shape[-1])
    grid = jnp.roll(tensor.reshape(slot_total, SIDE, SIDE, channel), (-SHIFT, -SHIFT), (1, 2))
    per_side = SIDE // WIN
    grid = grid.reshape(slot_total, per_side, WIN, per_side, WIN, channel).transpose(0, 1, 3, 2, 4, 5)
    return grid.reshape(slot_total, per_side * per_side, WIN * WIN, channel)

def from_windows(tensor):
    slot_total, channel = (tensor.shape[0], tensor.shape[-1])
    per_side = SIDE // WIN
    grid = tensor.reshape(slot_total, per_side, per_side, WIN, WIN, channel).transpose(0, 1, 3, 2, 4, 5)
    grid = jnp.roll(grid.reshape(slot_total, SIDE, SIDE, channel), (SHIFT, SHIFT), (1, 2))
    return grid.reshape(slot_total, SIDE * SIDE, channel)

def layer_norm(values, gain, offset):
    centred = values - lax.optimization_barrier(jnp.mean(values, -1, keepdims=True))
    inverse = lax.rsqrt(lax.optimization_barrier(jnp.mean(centred * centred, -1, keepdims=True)) + norm_eps)
    scaled = centred * inverse
    return (scaled * gain + offset, scaled, inverse)

def norm_back(grad_scaled, scaled, inverse):
    centre = lax.optimization_barrier(jnp.mean(grad_scaled, -1, keepdims=True))
    along = lax.optimization_barrier(jnp.mean(grad_scaled * scaled, -1, keepdims=True))
    return inverse * (grad_scaled - centre - scaled * along)

def gelu_value(inner):
    tangent = jnp.tanh(math.sqrt(2.0 / math.pi) * (inner + 0.044715 * inner * inner * inner))
    return 0.5 * inner * (1.0 + tangent)

def gelu_slope(inner):
    tangent = jnp.tanh(math.sqrt(2.0 / math.pi) * (inner + 0.044715 * inner * inner * inner))
    return 0.5 * (1.0 + tangent) + 0.5 * inner * (1.0 - tangent * tangent) * math.sqrt(2.0 / math.pi) * (1.0 + 3.0 * 0.044715 * inner * inner)

def product(spec, left, right):
    return jnp.einsum(spec, left.astype(jnp.float32), right.astype(jnp.float32))

def attend_block(block_images, block_upstream, slot_live, weights, vectors, hidden_bias, rel_table, onehot, blocked):
    qkv_weight, proj_weight, up_weight, down_weight = weights
    slot_total, token_total, feature_width = block_images.shape
    head_count = rel_table.shape[1]
    head_width = feature_width // head_count
    score_scale = head_width ** (-0.5)
    window_area = WIN * WIN
    row_total = slot_total * token_total
    row_live = jnp.broadcast_to(slot_live[:, None], (slot_total, token_total)).reshape(row_total, 1)
    inputs = block_images.reshape(row_total, feature_width).astype(jnp.float32)
    normed_first, scaled_first, inverse_first = layer_norm(inputs, vectors[0], vectors[1])
    normed_first = normed_first.astype(jnp.bfloat16)
    qkv_bias = jnp.concatenate([vectors[2], jnp.zeros_like(vectors[2]), vectors[3]])
    qkv_rows = (jnp.dot(normed_first, qkv_weight, preferred_element_type=jnp.float32) + qkv_bias).astype(jnp.bfloat16)
    windowed = to_windows(qkv_rows.reshape(slot_total, token_total, 3 * feature_width))
    windowed = windowed.reshape(slot_total, -1, window_area, 3, head_count, head_width)
    query_tokens = windowed[:, :, :, 0]
    key_tokens = windowed[:, :, :, 1]
    value_tokens = windowed[:, :, :, 2]
    position_bias = jnp.dot(onehot, rel_table, precision=lax.Precision.HIGHEST).T.reshape(head_count, window_area, window_area)

    def score_pass():
        raw = product('swihd,swjhd->swhij', query_tokens, key_tokens) * score_scale
        return raw + position_bias[None, None] + blocked[None, :, None]
    scores = score_pass()
    log_total = jnp.log(lax.optimization_barrier(jnp.sum(jnp.exp(scores), -1)))
    probs = jnp.exp(scores - log_total[..., None]).astype(jnp.bfloat16)
    mixed_win = product('swhij,swjhd->swihd', probs, value_tokens).astype(jnp.bfloat16)
    mixed_rows = from_windows(mixed_win.reshape(slot_total, -1, window_area, feature_width)).reshape(row_total, feature_width)
    residual = inputs + jnp.dot(mixed_rows, proj_weight, preferred_element_type=jnp.float32) + vectors[4]
    normed_second, scaled_second, inverse_second = layer_norm(residual, vectors[5], vectors[6])
    normed_second = normed_second.astype(jnp.bfloat16)
    preact = jnp.dot(normed_second, up_weight, preferred_element_type=jnp.float32) + hidden_bias
    hidden = gelu_value(preact).astype(jnp.bfloat16)
    final = residual + jnp.dot(hidden, down_weight, preferred_element_type=jnp.float32) + vectors[7]
    output = (final * row_live).astype(jnp.bfloat16).reshape(slot_total, token_total, feature_width)
    upstream = block_upstream.reshape(row_total, feature_width) * row_live.astype(jnp.bfloat16)
    upstream_float = upstream.astype(jnp.float32)
    down_grad = jnp.dot(hidden.T, upstream, preferred_element_type=jnp.float32)
    hidden_back = jnp.dot(upstream, down_weight.T, preferred_element_type=jnp.float32) * gelu_slope(preact)
    hidden_round = hidden_back.astype(jnp.bfloat16)
    up_grad = jnp.dot(normed_second.T, hidden_round, preferred_element_type=jnp.float32)
    norm_second_back = jnp.dot(hidden_round, up_weight.T, preferred_element_type=jnp.float32)
    resid_back = upstream_float + norm_back(norm_second_back * vectors[5], scaled_second, inverse_second)
    resid_round = resid_back.astype(jnp.bfloat16)
    proj_grad = jnp.dot(mixed_rows.T, resid_round, preferred_element_type=jnp.float32)
    mixed_back = jnp.dot(resid_round, proj_weight.T, preferred_element_type=jnp.float32).astype(jnp.bfloat16)
    mixed_back_win = to_windows(mixed_back.reshape(slot_total, token_total, feature_width))
    mixed_back_win = mixed_back_win.reshape(slot_total, -1, window_area, head_count, head_width)
    prob_full = jnp.exp(score_pass() - log_total[..., None])
    value_back = product('swhij,swihd->swjhd', probs, mixed_back_win)
    prob_back = product('swihd,swjhd->swhij', mixed_back_win, value_tokens)
    score_back = prob_full * (prob_back - lax.optimization_barrier(jnp.sum(prob_full * prob_back, -1, keepdims=True)))
    summed_scores = lax.optimization_barrier(jnp.sum(score_back, (0, 1))).reshape(head_count, window_area * window_area)
    table_grad = jnp.dot(summed_scores, onehot, precision=lax.Precision.HIGHEST).T
    score_round = score_back.astype(jnp.bfloat16)
    query_back = product('swhij,swjhd->swihd', score_round, key_tokens) * score_scale
    key_back = product('swhij,swihd->swjhd', score_round, query_tokens) * score_scale
    qkv_back_win = jnp.stack([query_back, key_back, value_back], 3).reshape(slot_total, -1, window_area, 3 * feature_width)
    qkv_back = from_windows(qkv_back_win).reshape(row_total, 3 * feature_width)
    qkv_round = qkv_back.astype(jnp.bfloat16)
    qkv_grad = jnp.dot(normed_first.T, qkv_round, preferred_element_type=jnp.float32)
    norm_first_back = jnp.dot(qkv_round, qkv_weight.T, preferred_element_type=jnp.float32)
    input_grad = resid_back + norm_back(norm_first_back * vectors[0], scaled_first, inverse_first)
    vector_grad = jnp.stack([lax.optimization_barrier(jnp.sum(norm_first_back * scaled_first, 0)), lax.optimization_barrier(jnp.sum(norm_first_back, 0)), lax.optimization_barrier(jnp.sum(qkv_back[:, :feature_width], 0)), lax.optimization_barrier(jnp.sum(qkv_back[:, 2 * feature_width:], 0)), lax.optimization_barrier(jnp.sum(resid_back, 0)), lax.optimization_barrier(jnp.sum(norm_second_back * scaled_second, 0)), lax.optimization_barrier(jnp.sum(norm_second_back, 0)), lax.optimization_barrier(jnp.sum(upstream_float, 0))])
    bias_grad = lax.optimization_barrier(jnp.sum(hidden_back, 0))
    input_grad = input_grad.reshape(slot_total, token_total, feature_width)
    return (output, input_grad, (qkv_grad, proj_grad, up_grad, down_grad), (vector_grad, bias_grad, table_grad))

def newton(current):
    for sweep in range(NS_STEPS):
        gram = jnp.dot(current, current.T, precision=lax.Precision.HIGHEST)
        poly = newton_second * gram + newton_third * jnp.dot(gram, gram, precision=lax.Precision.HIGHEST)
        current = newton_first * current + jnp.dot(poly, current, precision=lax.Precision.HIGHEST)
    return current

def muon(grad, weight, moment, flipped, factor):
    moment_new = muon_momentum * moment + grad
    start = moment_new.T if flipped else moment_new
    start = start / (jnp.sqrt(jnp.sum(start * start)) + frob_eps)
    ortho = newton(start)
    ortho = ortho.T if flipped else ortho
    return (weight - muon_rate * (factor * ortho + muon_decay * weight), moment_new)

def adam(grad, param, first, second):
    first_new = beta_first * first + (1.0 - beta_first) * grad
    second_new = beta_second * second + (1.0 - beta_second) * grad * grad
    first_hat = first_new / (1.0 - beta_first ** adam_count)
    second_hat = second_new / (1.0 - beta_second ** adam_count)
    return (param - adam_rate * first_hat / (jnp.sqrt(second_hat) + adam_eps), first_new, second_new)

def add_pair(first, second):
    return first + second

def reference(images, grad_output, live_count, qkv_weight, proj_weight, up_weight, down_weight, qkv_moment, proj_moment, up_moment, down_moment, vectors, hidden_bias, rel_table, vector_first, vector_second, bias_first, bias_second, table_first, table_second):
    onehot, blocked = window_tables(SIDE, WIN, SHIFT)
    device_total = live_count.size
    rounded = (qkv_weight.astype(jnp.bfloat16), proj_weight.astype(jnp.bfloat16), up_weight.astype(jnp.bfloat16), down_weight.astype(jnp.bfloat16))
    image_blocks = images.reshape(device_total, SLOTS, SIDE * SIDE, D)
    upstream_blocks = grad_output.reshape(device_total, SLOTS, SIDE * SIDE, D)
    live = (jnp.arange(SLOTS, dtype=jnp.int32)[None, :] < live_count.reshape(device_total, 1)).astype(jnp.float32)
    zero_big = (jnp.zeros((D, 3 * D), jnp.float32), jnp.zeros((D, D), jnp.float32), jnp.zeros((D, FF), jnp.float32), jnp.zeros((FF, D), jnp.float32))
    zero_small = (jnp.zeros((8, D), jnp.float32), jnp.zeros((FF,), jnp.float32), jnp.zeros(rel_table.shape, jnp.float32))

    def visit(carry, item):
        block_images, block_upstream, block_live = item
        out_block, back_block, big, small = attend_block(block_images, block_upstream, block_live, rounded, vectors, hidden_bias, rel_table, onehot, blocked)
        return (jax.tree.map(add_pair, carry, (big, small)), (out_block, back_block))
    totals, stacked = lax.scan(visit, (zero_big, zero_small), (image_blocks, upstream_blocks, live))
    big_sum, small_sum = totals
    output = stacked[0].reshape(images.shape)
    input_grad = stacked[1].reshape(images.shape)
    qkv_grad, proj_grad, up_grad, down_grad = big_sum
    vector_grad, bias_grad, table_grad = small_sum
    new_qkv, qkv_momentum = muon(qkv_grad, qkv_weight, qkv_moment, False, math.sqrt(3.0))
    new_proj, proj_momentum = muon(proj_grad, proj_weight, proj_moment, False, 1.0)
    new_up, up_momentum = muon(up_grad, up_weight, up_moment, False, math.sqrt(max(1.0, FF / D)))
    new_down, down_momentum = muon(down_grad, down_weight, down_moment, True, 1.0)
    new_vectors, vector_mean, vector_square = adam(vector_grad, vectors, vector_first, vector_second)
    new_bias, bias_mean, bias_square = adam(bias_grad, hidden_bias, bias_first, bias_second)
    new_table, table_mean, table_square = adam(table_grad, rel_table, table_first, table_second)
    return (output, input_grad, qkv_grad, proj_grad, up_grad, down_grad, vector_grad, bias_grad, table_grad, new_qkv, new_proj, new_up, new_down, qkv_momentum, proj_momentum, up_momentum, down_momentum, new_vectors, new_bias, new_table, vector_mean, vector_square, bias_mean, bias_square, table_mean, table_square)
```

```python
import functools
import math

import jax
import jax.numpy as jnp
import numpy as np
from jax import lax
from jax.experimental import pallas as pl
from jax.experimental.pallas import tpu as pltpu
from jax.sharding import PartitionSpec as P

D = 512
FF = 2048
SIDE = 14
WIN = 7
SHIFT = 3
NS_STEPS = 5


norm_eps = 1e-05
mask_fill = -100.0
muon_momentum = 0.95
muon_rate = 0.4
muon_decay = 0.1
adam_rate = 0.1
beta_first = 0.9
beta_second = 0.999
adam_eps = 1e-08
adam_count = 10.0
frob_eps = 1e-06
newton_first = 3.4445
newton_second = -4.775
newton_third = 2.0315


def window_tables(side, window, shift):
    steps = np.arange(window)
    row_pos = np.repeat(steps, window)
    col_pos = np.tile(steps, window)
    span = 2 * window - 1
    offset = (row_pos[:, None] - row_pos[None, :] + window - 1) * span + (
        col_pos[:, None] - col_pos[None, :] + window - 1
    )
    onehot = (offset.reshape(-1)[:, None] == np.arange(span * span)[None, :]).astype(np.float32)
    line = np.arange(side)
    label = (line >= side - window).astype(np.int64) + (line >= side - shift).astype(np.int64)
    region = 3 * label[:, None] + label[None, :]
    per_side = side // window
    region = (
        region.reshape(per_side, window, per_side, window)
        .transpose(0, 2, 1, 3)
        .reshape(per_side * per_side, window * window)
    )
    blocked = np.where(region[:, :, None] != region[:, None, :], mask_fill, 0.0).astype(np.float32)
    return (jnp.asarray(onehot), jnp.asarray(blocked))


def to_windows(tensor):
    slot_total, channel = (tensor.shape[0], tensor.shape[-1])
    grid = jnp.roll(tensor.reshape(slot_total, SIDE, SIDE, channel), (-SHIFT, -SHIFT), (1, 2))
    per_side = SIDE // WIN
    grid = grid.reshape(slot_total, per_side, WIN, per_side, WIN, channel).transpose(
        0, 1, 3, 2, 4, 5
    )
    return grid.reshape(slot_total, per_side * per_side, WIN * WIN, channel)


def from_windows(tensor):
    slot_total, channel = (tensor.shape[0], tensor.shape[-1])
    per_side = SIDE // WIN
    grid = tensor.reshape(slot_total, per_side, per_side, WIN, WIN, channel).transpose(
        0, 1, 3, 2, 4, 5
    )
    grid = jnp.roll(grid.reshape(slot_total, SIDE, SIDE, channel), (SHIFT, SHIFT), (1, 2))
    return grid.reshape(slot_total, SIDE * SIDE, channel)


def layer_norm(values, gain, offset):
    centred = values - jnp.mean(values, -1, keepdims=True)
    inverse = lax.rsqrt(jnp.mean(centred * centred, -1, keepdims=True) + norm_eps)
    scaled = centred * inverse
    return (scaled * gain + offset, scaled, inverse)


def norm_back(grad_scaled, scaled, inverse):
    centre = jnp.mean(grad_scaled, -1, keepdims=True)
    along = jnp.mean(grad_scaled * scaled, -1, keepdims=True)
    return inverse * (grad_scaled - centre - scaled * along)


def gelu_value(inner):
    tangent = jnp.tanh(math.sqrt(2.0 / math.pi) * (inner + 0.044715 * inner * inner * inner))
    return 0.5 * inner * (1.0 + tangent)


def gelu_slope(inner):
    tangent = jnp.tanh(math.sqrt(2.0 / math.pi) * (inner + 0.044715 * inner * inner * inner))
    return 0.5 * (1.0 + tangent) + 0.5 * inner * (1.0 - tangent * tangent) * math.sqrt(
        2.0 / math.pi
    ) * (1.0 + 3.0 * 0.044715 * inner * inner)


def product(spec, left, right):
    return jnp.einsum(spec, left, right, preferred_element_type=jnp.float32)


def attend_block(
    block_images,
    block_upstream,
    slot_live,
    qkv_weight,
    proj_weight,
    up_weight,
    down_weight,
    vectors,
    hidden_bias,
    rel_table,
    onehot,
    blocked,
):
    slot_total, token_total, feature_width = block_images.shape
    head_count = rel_table.shape[1]
    head_width = feature_width // head_count
    score_scale = head_width ** (-0.5)
    window_area = WIN * WIN
    row_total = slot_total * token_total
    row_live = jnp.broadcast_to(slot_live[:, None], (slot_total, token_total)).reshape(row_total, 1)
    inputs = block_images.reshape(row_total, feature_width).astype(jnp.float32)
    normed_first, scaled_first, inverse_first = layer_norm(inputs, vectors[0], vectors[1])
    normed_first = normed_first.astype(jnp.bfloat16)
    qkv_bias = jnp.concatenate([vectors[2], jnp.zeros_like(vectors[2]), vectors[3]])
    qkv_rows = (
        jnp.dot(normed_first, qkv_weight, preferred_element_type=jnp.float32) + qkv_bias
    ).astype(jnp.bfloat16)
    windowed = to_windows(qkv_rows.reshape(slot_total, token_total, 3 * feature_width))
    windowed = windowed.reshape(slot_total, -1, window_area, 3, head_count, head_width)
    query_tokens = windowed[:, :, :, 0]
    key_tokens = windowed[:, :, :, 1]
    value_tokens = windowed[:, :, :, 2]
    position_bias = jnp.dot(onehot, rel_table, precision=lax.Precision.HIGHEST).T.reshape(
        head_count, window_area, window_area
    )

    def score_pass():
        raw = product("swihd,swjhd->swhij", query_tokens, key_tokens) * score_scale
        return raw + position_bias[None, None] + blocked[None, :, None]

    scores = score_pass()
    log_total = jnp.log(jnp.sum(jnp.exp(scores), -1))
    probs = jnp.exp(scores - log_total[..., None]).astype(jnp.bfloat16)
    mixed_win = product("swhij,swjhd->swihd", probs, value_tokens).astype(jnp.bfloat16)
    mixed_rows = from_windows(
        mixed_win.reshape(slot_total, -1, window_area, feature_width)
    ).reshape(row_total, feature_width)
    residual = (
        inputs + jnp.dot(mixed_rows, proj_weight, preferred_element_type=jnp.float32) + vectors[4]
    )
    normed_second, scaled_second, inverse_second = layer_norm(residual, vectors[5], vectors[6])
    normed_second = normed_second.astype(jnp.bfloat16)
    preact = jnp.dot(normed_second, up_weight, preferred_element_type=jnp.float32) + hidden_bias
    hidden = gelu_value(preact).astype(jnp.bfloat16)
    final = residual + jnp.dot(hidden, down_weight, preferred_element_type=jnp.float32) + vectors[7]
    output = (final * row_live).astype(jnp.bfloat16).reshape(slot_total, token_total, feature_width)
    upstream = block_upstream.reshape(row_total, feature_width) * row_live.astype(jnp.bfloat16)
    upstream_float = upstream.astype(jnp.float32)
    down_grad = jnp.dot(hidden.T, upstream, preferred_element_type=jnp.float32)
    hidden_back = jnp.dot(upstream, down_weight.T, preferred_element_type=jnp.float32) * gelu_slope(
        preact
    )
    hidden_round = hidden_back.astype(jnp.bfloat16)
    up_grad = jnp.dot(normed_second.T, hidden_round, preferred_element_type=jnp.float32)
    norm_second_back = jnp.dot(hidden_round, up_weight.T, preferred_element_type=jnp.float32)
    resid_back = upstream_float + norm_back(
        norm_second_back * vectors[5], scaled_second, inverse_second
    )
    resid_round = resid_back.astype(jnp.bfloat16)
    proj_grad = jnp.dot(mixed_rows.T, resid_round, preferred_element_type=jnp.float32)
    mixed_back = jnp.dot(resid_round, proj_weight.T, preferred_element_type=jnp.float32).astype(
        jnp.bfloat16
    )
    mixed_back_win = to_windows(mixed_back.reshape(slot_total, token_total, feature_width))
    mixed_back_win = mixed_back_win.reshape(slot_total, -1, window_area, head_count, head_width)
    prob_full = jnp.exp(score_pass() - log_total[..., None])
    value_back = product("swhij,swihd->swjhd", probs, mixed_back_win)
    prob_back = product("swihd,swjhd->swhij", mixed_back_win, value_tokens)
    score_back = prob_full * (prob_back - jnp.sum(prob_full * prob_back, -1, keepdims=True))
    summed_scores = jnp.sum(score_back, (0, 1)).reshape(head_count, window_area * window_area)
    table_grad = jnp.dot(summed_scores, onehot, precision=lax.Precision.HIGHEST).T
    score_round = score_back.astype(jnp.bfloat16)
    query_back = product("swhij,swjhd->swihd", score_round, key_tokens) * score_scale
    key_back = product("swhij,swihd->swjhd", score_round, query_tokens) * score_scale
    qkv_back_win = jnp.stack([query_back, key_back, value_back], 3).reshape(
        slot_total, -1, window_area, 3 * feature_width
    )
    qkv_back = from_windows(qkv_back_win).reshape(row_total, 3 * feature_width)
    qkv_round = qkv_back.astype(jnp.bfloat16)
    qkv_grad = jnp.dot(normed_first.T, qkv_round, preferred_element_type=jnp.float32)
    norm_first_back = jnp.dot(qkv_round, qkv_weight.T, preferred_element_type=jnp.float32)
    input_grad = resid_back + norm_back(norm_first_back * vectors[0], scaled_first, inverse_first)
    vector_grad = jnp.stack(
        [
            jnp.sum(norm_first_back * scaled_first, 0),
            jnp.sum(norm_first_back, 0),
            jnp.sum(qkv_back[:, :feature_width], 0),
            jnp.sum(qkv_back[:, 2 * feature_width :], 0),
            jnp.sum(resid_back, 0),
            jnp.sum(norm_second_back * scaled_second, 0),
            jnp.sum(norm_second_back, 0),
            jnp.sum(upstream_float, 0),
        ]
    )
    bias_grad = jnp.sum(hidden_back, 0)
    input_grad = input_grad.reshape(slot_total, token_total, feature_width)
    return (
        output,
        input_grad,
        qkv_grad,
        proj_grad,
        up_grad,
        down_grad,
        vector_grad,
        bias_grad,
        table_grad,
    )


BF = jnp.bfloat16
F32 = jnp.float32
HALF = D // 2
PART = D // 8


def shape(dims, kind):
    return jax.ShapeDtypeStruct(tuple(dims), kind)


def run(kernel, name, places, args, outs, scratch=(), flops=0):
    vmem = pl.BlockSpec(memory_space=pltpu.VMEM)
    moved = sum((int(np.prod(item.shape)) * item.dtype.itemsize for item in [*args, *outs]))
    return pl.pallas_call(
        kernel,
        out_shape=list(outs),
        in_specs=[pl.BlockSpec(memory_space=pltpu.SMEM)] + [vmem] * len(args),
        out_specs=[vmem] * len(outs),
        scratch_shapes=list(scratch),
        name=name,
        cost_estimate=pl.CostEstimate(flops=flops, bytes_accessed=moved, transcendentals=0),
        compiler_params=pltpu.CompilerParams(vmem_limit_bytes=62 * 1024 * 1024),
    )(places, *args)


def rows_at(start, size):
    return pl.ds(pl.multiple_of(start, size), size)


def prep_kernel(place, wq, wp, wu, wd, mq, mp, mu, md, sa, sb, pa, pb, mom, flip):
    ug, qg = (wu.shape[1], wq.shape[1])
    core, chip = (place[0], place[1])
    sb[:, :qg] = wq[...].astype(BF)
    sb[:, qg:] = wp[...].astype(BF)
    sa[:, :ug] = wu[...].astype(BF)
    sa[:, ug:] = wd[...].T.astype(BF)
    for half in range(2):
        bit = (chip >> half) & 1
        source = rows_at(half * HALF + (bit * 2 + core) * PART, PART)
        pa[half * PART : (half + 1) * PART, :] = sa[source, :]
        pb[half * PART : (half + 1) * PART, :] = sb[source, :]
    flip[...] = md[...].T
    piece = mom.shape[0]
    source = rows_at(core * HALF + chip * piece, piece)
    mom[:, :ug] = mu[source, :]
    mom[:, ug : 2 * ug] = flip[source, :]
    mom[:, 2 * ug : 2 * ug + qg] = mq[source, :]
    mom[:, 2 * ug + qg :] = mp[source, :]


def join_kernel(group_count, widths, place, *refs):
    core, chip, zone = (place[0], place[1], place[2])
    far = group_count - 1
    own = refs[0]
    mine = refs[1 : 1 + far] + refs[1 + far : 3 + far]
    theirs = refs[3 + far : 3 + 2 * far] + refs[3 + 2 * far : 5 + 2 * far]
    outs = refs[5 + 2 * far :]
    offset = 0
    for out, width in zip(outs, widths):
        span = slice(offset, offset + width)
        out[:, rows_at(zone * width, width)] = own[:, span]
        for step in range(1, group_count):
            columns = rows_at((zone ^ step) * width, width)
            for parts, seat in ((mine, core), (theirs, 1 - core)):
                for half in range(2):
                    bit = (chip >> half) & 1
                    base = half * HALF
                    near = parts[step - 1][half * PART : (half + 1) * PART, span]
                    out[rows_at(base + (bit * 2 + seat) * PART, PART), columns] = near
                    swap = parts[far + half][(step - 1) * PART : step * PART, span]
                    out[rows_at(base + ((1 - bit) * 2 + seat) * PART, PART), columns] = swap
        offset += width


def halve_kernel(place, keep, came, own, *sends):
    chip = place[1]
    piece = own.shape[0]

    def total(step):
        source = rows_at((chip ^ step) * piece, piece)
        return keep[source, :].astype(F32) + came[source, :].astype(F32)

    own[...] = total(0)
    for step, send in enumerate(sends):
        send[...] = total(step + 1).astype(BF)


def plane_kernel(chips, place, *refs):
    zone = place[2]
    own, came, outs = (refs[0], refs[1:chips], refs[chips:])
    width = outs[0].shape[1]

    def total(step):
        columns = rows_at((zone ^ step) * width, width)
        value = own[:, columns]
        for item in came:
            value = value + item[:, columns].astype(F32)
        return value

    outs[0][...] = total(0)
    for step in range(1, len(outs)):
        outs[step][...] = total(step).astype(BF)


def momentum_kernel(group_count, qg, place, *refs):
    zone = place[2]
    first = refs[:group_count]
    second = refs[group_count : 2 * group_count]
    mom, piece = refs[2 * group_count : 2 * group_count + 2]
    outs, slots = (refs[2 * group_count + 2 : -1], refs[-1])
    ug = slots.shape[2]

    def total(parts):
        value = parts[0][...]
        for item in parts[1:]:
            value = value + item[...].astype(F32)
        return value

    one, two = (total(first), total(second))
    piece[:, : 2 * ug] = one.astype(BF)
    piece[:, 2 * ug :] = two.astype(BF)
    one = muon_momentum * mom[:, : 2 * ug] + one
    two = muon_momentum * mom[:, 2 * ug :] + two
    slots[...] = jnp.zeros_like(slots)
    slots[0] = one[:, :ug].astype(BF)
    slots[1] = one[:, ug:].astype(BF)
    slots[2, :, :qg] = two[:, :qg].astype(BF)
    slots[3, :, : two.shape[1] - qg] = two[:, qg:].astype(BF)
    for step in range(group_count):
        outs[step][...] = slots[zone ^ step]


def split(value):
    high = value.astype(BF)
    return (high, (value - high.astype(F32)).astype(BF))


def dot32(left, right):
    return jnp.dot(left, right, preferred_element_type=F32)


def triple(left, right):
    return dot32(left[0], right[0]) + (dot32(left[0], right[1]) + dot32(left[1], right[0]))


def newton_kernel(count, place, *refs):
    parts, outs = (refs[:count], refs[count:-3])
    whole, gram, lead = refs[-3:]
    piece = parts[0].shape[0]
    for step, item in enumerate(parts):
        whole[step * piece : (step + 1) * piece, :] = item[...]
    matrix = whole[...]
    raw = lax.dot_general(matrix, matrix, (((1,), (1,)), ((), ())), preferred_element_type=F32)
    row = lax.broadcasted_iota(jnp.int32, raw.shape, 0)
    column = lax.broadcasted_iota(jnp.int32, raw.shape, 1)
    norm = jnp.sqrt(jnp.sum(jnp.where(row == column, raw, 0.0), keepdims=True))
    scale = 1.0 / (norm + frob_eps)
    gram[...] = raw * (scale * scale)
    lead[...] = jnp.where(row[:piece] == column[:piece], scale, 0.0)

    def sweep(index, carry):
        now = gram[...]
        pair = split(now)
        square = triple(pair, pair)
        poly = newton_second * now + newton_third * square
        front = lead[...]
        turn = split(poly)
        lead[...] = newton_first * front + triple(split(front), turn)
        mixed = newton_first * now + triple(turn, pair)
        gram[...] = newton_first * mixed + triple(turn, split(mixed))
        return carry

    lax.fori_loop(0, NS_STEPS - 1, sweep, 0)
    pair = split(gram[...])
    front = lead[...]
    once = triple(split(front), pair)
    twice = newton_second * front + newton_third * once
    front = newton_first * front + triple(split(twice), pair)
    high, low = split(front)
    width = outs[0].shape[1]
    for step, out in enumerate(outs):
        block = whole[:, step * width : (step + 1) * width]
        out[...] = (dot32(high, block) + dot32(low, block)).astype(BF)


def pack_kernel(group_count, qg, place, *refs):
    zone = place[2]
    out, stack = refs[group_count:]
    ug = stack.shape[2]
    for step in range(group_count):
        stack[step] = refs[step][...]
    out[:, :ug] = stack[zone]
    out[:, ug : 2 * ug] = stack[zone ^ 1]
    out[:, 2 * ug : 2 * ug + qg] = stack[zone ^ 2][:, :qg]
    out[:, 2 * ug + qg :] = stack[zone ^ 3][:, : out.shape[1] - 2 * ug - qg]


def spread(place, parts, ref, span):
    core, chip = (place[0], place[1])
    piece = parts[0].shape[0]
    near = len(parts) // 2
    for step, part in enumerate(parts):
        seat = core if step < near else 1 - core
        ref[rows_at(seat * HALF + (chip ^ (step % near)) * piece, piece), :] = part[:, span].astype(
            F32
        )


def grad_kernel(count, place, *refs):
    parts = refs[:count]
    mq, mp, mu, md = refs[count : count + 4]
    gq, gp, gu, gd, nq, np_, nu, nd, flip = refs[count + 4 :]
    ug, qg = (gu.shape[1], gq.shape[1])
    spread(place, parts, gu, slice(0, ug))
    spread(place, parts, flip, slice(ug, 2 * ug))
    spread(place, parts, gq, slice(2 * ug, 2 * ug + qg))
    spread(place, parts, gp, slice(2 * ug + qg, None))
    gd[...] = flip[...].T
    nq[...] = muon_momentum * mq[...] + gq[...]
    np_[...] = muon_momentum * mp[...] + gp[...]
    nu[...] = muon_momentum * mu[...] + gu[...]
    nd[...] = muon_momentum * md[...] + gd[...]


def weight_kernel(count, place, *refs):
    parts = refs[:count]
    wq, wp, wu, wd = refs[count : count + 4]
    nq, np_, nu, nd, flip = refs[count + 4 :]
    ug, qg = (nu.shape[1], nq.shape[1])
    spread(place, parts, nu, slice(0, ug))
    spread(place, parts, flip, slice(ug, 2 * ug))
    spread(place, parts, nq, slice(2 * ug, 2 * ug + qg))
    spread(place, parts, np_, slice(2 * ug + qg, None))
    for new, old, factor in (
        (nq, wq, math.sqrt(3.0)),
        (np_, wp, 1.0),
        (nu, wu, math.sqrt(max(1.0, FF / D))),
    ):
        new[...] = old[...] - muon_rate * (factor * new[...] + muon_decay * old[...])
    nd[...] = wd[...] - muon_rate * (flip[...].T + muon_decay * wd[...])


def adam(grad, param, first, second):
    first_new = beta_first * first + (1.0 - beta_first) * grad
    second_new = beta_second * second + (1.0 - beta_second) * grad * grad
    first_hat = first_new / (1.0 - beta_first**adam_count)
    second_hat = second_new / (1.0 - beta_second**adam_count)
    return (
        param - adam_rate * first_hat / (jnp.sqrt(second_hat) + adam_eps),
        first_new,
        second_new,
    )


def local(
    images,
    grad_output,
    live_count,
    qkv_weight,
    proj_weight,
    up_weight,
    down_weight,
    qkv_moment,
    proj_moment,
    up_moment,
    down_moment,
    vectors,
    hidden_bias,
    rel_table,
    vector_first,
    vector_second,
    bias_first,
    bias_second,
    table_first,
    table_second,
):
    onehot, blocked = window_tables(SIDE, WIN, SHIFT)
    groups, members = (lax.axis_size("group"), lax.axis_size("dp"))
    chips = members // 2
    piece = D // members
    seat, zone = (lax.axis_index("dp"), lax.axis_index("group"))
    place = jnp.stack([seat & 1, seat >> 1, zone, seat]).astype(jnp.int32)
    ug, qg, pg = (up_weight.shape[1], qkv_weight.shape[1], proj_weight.shape[1])

    def zshift(value, step):
        return lax.ppermute(value, "group", [(item, item ^ step) for item in range(groups)])

    def dshift(value, step):
        return lax.ppermute(value, "dp", [(item, item ^ step) for item in range(members)])

    shard_up, shard_qkv, part_up, part_qkv, moment_rows = run(
        prep_kernel,
        "prep",
        place,
        [
            qkv_weight,
            proj_weight,
            up_weight,
            down_weight,
            qkv_moment,
            proj_moment,
            up_moment,
            down_moment,
        ],
        [
            shape((D, 2 * ug), BF),
            shape((D, qg + pg), BF),
            shape((2 * PART, 2 * ug), BF),
            shape((2 * PART, qg + pg), BF),
            shape((piece, 2 * ug + qg + pg), F32),
        ],
        [pltpu.VMEM((D, ug), F32)],
    )

    def gather(shard, part, widths, name):
        far = [zshift(part, step) for step in range(1, groups)]
        across = dshift(jnp.concatenate([item[:PART] for item in far]), 2)
        along = dshift(jnp.concatenate([item[PART:] for item in far]), 4)
        mine = far + [across, along]
        theirs = [dshift(item, 1) for item in mine]
        fits = all((width % 128 == 0 for width in widths))
        kept = widths if fits else (sum(widths),)
        joined = run(
            functools.partial(join_kernel, groups, kept),
            name,
            place,
            [shard, *mine, *theirs],
            [shape((D, groups * width), BF) for width in kept],
        )
        if fits:
            return joined
        joined = joined[0].reshape(D, groups, -1)
        cut = widths[0]
        return [joined[:, :, :cut].reshape(D, -1), joined[:, :, cut:].reshape(D, -1)]

    full_qkv, full_proj = gather(shard_qkv, part_qkv, (qg, pg), "join_qkv")
    full_up, full_flip = gather(shard_up, part_up, (ug, ug), "join_up")
    slot_live = (jnp.arange(images.shape[0], dtype=jnp.int32) < live_count.reshape(())).astype(
        jnp.float32
    )
    (
        output,
        input_grad,
        local_qkv,
        local_proj,
        local_up,
        local_down,
        local_vector,
        local_bias,
        local_table,
    ) = attend_block(
        images,
        grad_output,
        slot_live,
        full_qkv,
        full_proj,
        full_up,
        full_flip.T,
        vectors,
        hidden_bias,
        rel_table,
        onehot,
        blocked,
    )

    def blocks(left, right):
        pair = [item.astype(BF).reshape(D, groups, -1) for item in (left, right)]
        return jnp.concatenate(pair, 2).reshape(D, -1)

    def reduce(grads, name):
        keep = lax.dynamic_slice_in_dim(grads, place[0] * HALF, HALF)
        send = lax.dynamic_slice_in_dim(grads, (1 - place[0]) * HALF, HALF)
        width = grads.shape[1]
        own, *sends = run(
            halve_kernel,
            "halve_" + name,
            place,
            [keep, dshift(send, 1)],
            [shape((piece, width), F32)] + [shape((piece, width), BF)] * (chips - 1),
        )
        came = [dshift(item, 2 * (step + 1)) for step, item in enumerate(sends)]
        width = width // groups
        own, *sends = run(
            functools.partial(plane_kernel, chips),
            "plane_" + name,
            place,
            [own, *came],
            [shape((piece, width), F32)] + [shape((piece, width), BF)] * (groups - 1),
        )
        return [own] + [zshift(item, step + 1) for step, item in enumerate(sends)]

    first = reduce(blocks(local_up, local_down.T), "up")
    second = reduce(blocks(local_qkv, local_proj), "qkv")
    grad_piece, *outgoing = run(
        functools.partial(momentum_kernel, groups, qg),
        "momentum",
        place,
        [*first, *second, moment_rows],
        [shape((piece, 2 * ug + qg + pg), BF)] + [shape((piece, ug), BF)] * groups,
        [pltpu.VMEM((max(groups, 4), piece, ug), BF)],
    )

    def share(value):
        near = [value] + [dshift(value, 2 * step) for step in range(1, chips)]
        return near + [dshift(item, 1) for item in near]

    owned = [outgoing[0]] + [zshift(outgoing[step], step) for step in range(1, groups)]
    everyone = share(jnp.concatenate(owned, 1))
    results = run(
        functools.partial(newton_kernel, members),
        "newton",
        place,
        everyone,
        [shape((piece, ug), BF)] * groups,
        [
            pltpu.VMEM((D, groups * ug), BF),
            pltpu.VMEM((D, D), F32),
            pltpu.VMEM((piece, D), F32),
        ],
    )
    back = [results[0]] + [zshift(results[step], step) for step in range(1, groups)]
    (packed,) = run(
        functools.partial(pack_kernel, groups, qg),
        "pack",
        place,
        back,
        [shape((piece, 2 * ug + qg + pg), BF)],
        [pltpu.VMEM((groups, piece, ug), BF)],
    )
    mats = [(D, qg), (D, pg), (D, ug), (ug, D)]
    (
        qkv_grad,
        proj_grad,
        up_grad,
        down_grad,
        qkv_momentum,
        proj_momentum,
        up_momentum,
        down_momentum,
    ) = run(
        functools.partial(grad_kernel, members),
        "grads",
        place,
        [*share(grad_piece), qkv_moment, proj_moment, up_moment, down_moment],
        [shape(item, F32) for item in mats + mats],
        [pltpu.VMEM((D, ug), F32)],
    )
    new_qkv, new_proj, new_up, new_down = run(
        functools.partial(weight_kernel, members),
        "weights",
        place,
        [*share(packed), qkv_weight, proj_weight, up_weight, down_weight],
        [shape(item, F32) for item in mats],
        [pltpu.VMEM((D, ug), F32)],
    )
    small = jnp.concatenate(
        [local_vector.reshape(-1), local_bias.reshape(-1), local_table.reshape(-1)]
    )
    pad = -small.size % 1024
    total = jnp.pad(small, (0, pad)).reshape(-1, 128)
    step = 1
    while step < members:
        total = total + dshift(total, step)
        step *= 2
    step = 1
    while step < groups:
        total = total + zshift(total, step)
        step *= 2
    total = total.reshape(-1)
    ends = np.cumsum([local_vector.size, local_bias.size, local_table.size])
    vector_grad = total[: ends[0]].reshape(local_vector.shape)
    bias_grad = total[ends[0] : ends[1]].reshape(local_bias.shape)
    table_grad = total[ends[1] : ends[2]].reshape(local_table.shape)
    new_vectors, vector_mean, vector_square = adam(
        vector_grad, vectors, vector_first, vector_second
    )
    new_bias, bias_mean, bias_square = adam(bias_grad, hidden_bias, bias_first, bias_second)
    new_table, table_mean, table_square = adam(table_grad, rel_table, table_first, table_second)
    return (
        output,
        input_grad,
        qkv_grad,
        proj_grad,
        up_grad,
        down_grad,
        vector_grad,
        bias_grad,
        table_grad,
        new_qkv,
        new_proj,
        new_up,
        new_down,
        qkv_momentum,
        proj_momentum,
        up_momentum,
        down_momentum,
        new_vectors,
        new_bias,
        new_table,
        vector_mean,
        vector_square,
        bias_mean,
        bias_square,
        table_mean,
        table_square,
    )


def solution(mesh):
    placed = (
        P(("dp", "group"), None, None),
        P(("dp", "group"), None, None),
        P("dp", "group"),
        P(None, "group"),
        P(None, "group"),
        P(None, "group"),
        P("group", None),
        P(None, "group"),
        P(None, "group"),
        P(None, "group"),
        P("group", None),
        P(),
        P(),
        P(),
        P(),
        P(),
        P(),
        P(),
        P(),
        P(),
    )
    return jax.shard_map(
        local,
        mesh=mesh,
        in_specs=placed,
        out_specs=(
            P(("dp", "group"), None, None),
            P(("dp", "group"), None, None),
            P(None, "group"),
            P(None, "group"),
            P(None, "group"),
            P("group", None),
            P(),
            P(),
            P(),
            P(None, "group"),
            P(None, "group"),
            P(None, "group"),
            P("group", None),
            P(None, "group"),
            P(None, "group"),
            P(None, "group"),
            P("group", None),
            P(),
            P(),
            P(),
            P(),
            P(),
            P(),
            P(),
            P(),
            P(),
        ),
        check_vma=False,
    )
```

```python
import functools
import math

import jax
import jax.numpy as jnp
import numpy as np
from jax import lax
from jax.experimental import pallas as pl
from jax.experimental.pallas import tpu as pltpu
from jax.sharding import PartitionSpec as P

D = 512
FF = 2048
SIDE = 14
WIN = 7
SHIFT = 3
NS_STEPS = 5


norm_eps = 1e-05
mask_fill = -100.0
muon_momentum = 0.95
muon_rate = 0.4
muon_decay = 0.1
adam_rate = 0.1
beta_first = 0.9
beta_second = 0.999
adam_eps = 1e-08
adam_count = 10.0
frob_eps = 1e-06
newton_first = 3.4445
newton_second = -4.775
newton_third = 2.0315


def window_tables(side, window, shift):
    steps = np.arange(window)
    row_pos = np.repeat(steps, window)
    col_pos = np.tile(steps, window)
    span = 2 * window - 1
    offset = (row_pos[:, None] - row_pos[None, :] + window - 1) * span + (
        col_pos[:, None] - col_pos[None, :] + window - 1
    )
    onehot = (offset.reshape(-1)[:, None] == np.arange(span * span)[None, :]).astype(np.float32)
    line = np.arange(side)
    label = (line >= side - window).astype(np.int64) + (line >= side - shift).astype(np.int64)
    region = 3 * label[:, None] + label[None, :]
    per_side = side // window
    region = (
        region.reshape(per_side, window, per_side, window)
        .transpose(0, 2, 1, 3)
        .reshape(per_side * per_side, window * window)
    )
    blocked = np.where(region[:, :, None] != region[:, None, :], mask_fill, 0.0).astype(np.float32)
    return (jnp.asarray(onehot), jnp.asarray(blocked))


def norm_back(grad_scaled, scaled, inverse):
    centre = jnp.mean(grad_scaled, -1, keepdims=True)
    along = jnp.mean(grad_scaled * scaled, -1, keepdims=True)
    return inverse * (grad_scaled - centre - scaled * along)


BF = jnp.bfloat16
F32 = jnp.float32
HALF = D // 2
PART = D // 8


def shape(dims, kind):
    return jax.ShapeDtypeStruct(tuple(dims), kind)


def run(kernel, name, places, args, outs, scratch=(), flops=0):
    vmem = pl.BlockSpec(memory_space=pltpu.VMEM)
    moved = sum((int(np.prod(item.shape)) * item.dtype.itemsize for item in [*args, *outs]))
    return pl.pallas_call(
        kernel,
        out_shape=list(outs),
        in_specs=[pl.BlockSpec(memory_space=pltpu.SMEM)] + [vmem] * len(args),
        out_specs=[vmem] * len(outs),
        scratch_shapes=list(scratch),
        name=name,
        cost_estimate=pl.CostEstimate(flops=flops, bytes_accessed=moved, transcendentals=0),
        compiler_params=pltpu.CompilerParams(vmem_limit_bytes=62 * 1024 * 1024),
    )(places, *args)


def rows_at(start, size):
    return pl.ds(pl.multiple_of(start, size), size)


def prep_kernel(place, wq, wp, wu, wd, mq, mp, mu, md, sa, sb, pa, pb, mom, flip):
    ug, qg = (wu.shape[1], wq.shape[1])
    core, chip = (place[0], place[1])
    sb[:, :qg] = wq[...].astype(BF)
    sb[:, qg:] = wp[...].astype(BF)
    sa[:, :ug] = wu[...].astype(BF)
    sa[:, ug:] = wd[...].T.astype(BF)
    for half in range(2):
        bit = (chip >> half) & 1
        source = rows_at(half * HALF + (bit * 2 + core) * PART, PART)
        pa[half * PART : (half + 1) * PART, :] = sa[source, :]
        pb[half * PART : (half + 1) * PART, :] = sb[source, :]
    flip[...] = md[...].T
    piece = mom.shape[0]
    source = rows_at(core * HALF + chip * piece, piece)
    mom[:, :ug] = mu[source, :]
    mom[:, ug : 2 * ug] = flip[source, :]
    mom[:, 2 * ug : 2 * ug + qg] = mq[source, :]
    mom[:, 2 * ug + qg :] = mp[source, :]


def join_kernel(group_count, widths, place, *refs):
    core, chip, zone = (place[0], place[1], place[2])
    far = group_count - 1
    own = refs[0]
    mine = refs[1 : 1 + far] + refs[1 + far : 3 + far]
    theirs = refs[3 + far : 3 + 2 * far] + refs[3 + 2 * far : 5 + 2 * far]
    outs = refs[5 + 2 * far :]
    offset = 0
    for out, width in zip(outs, widths):
        span = slice(offset, offset + width)
        out[:, rows_at(zone * width, width)] = own[:, span]
        for step in range(1, group_count):
            columns = rows_at((zone ^ step) * width, width)
            for parts, seat in ((mine, core), (theirs, 1 - core)):
                for half in range(2):
                    bit = (chip >> half) & 1
                    base = half * HALF
                    near = parts[step - 1][half * PART : (half + 1) * PART, span]
                    out[rows_at(base + (bit * 2 + seat) * PART, PART), columns] = near
                    swap = parts[far + half][(step - 1) * PART : step * PART, span]
                    out[rows_at(base + ((1 - bit) * 2 + seat) * PART, PART), columns] = swap
        offset += width


def halve_kernel(place, keep, came, own, *sends):
    chip = place[1]
    piece = own.shape[0]

    def total(step):
        source = rows_at((chip ^ step) * piece, piece)
        return keep[source, :].astype(F32) + came[source, :].astype(F32)

    own[...] = total(0)
    for step, send in enumerate(sends):
        send[...] = total(step + 1).astype(BF)


def plane_kernel(chips, place, *refs):
    zone = place[2]
    own, came, outs = (refs[0], refs[1:chips], refs[chips:])
    width = outs[0].shape[1]

    def total(step):
        columns = rows_at((zone ^ step) * width, width)
        value = own[:, columns]
        for item in came:
            value = value + item[:, columns].astype(F32)
        return value

    outs[0][...] = total(0)
    for step in range(1, len(outs)):
        outs[step][...] = total(step).astype(BF)


def momentum_kernel(group_count, qg, place, *refs):
    zone = place[2]
    first = refs[:group_count]
    second = refs[group_count : 2 * group_count]
    mom, piece = refs[2 * group_count : 2 * group_count + 2]
    outs, slots = (refs[2 * group_count + 2 : -1], refs[-1])
    ug = slots.shape[2]

    def total(parts):
        value = parts[0][...]
        for item in parts[1:]:
            value = value + item[...].astype(F32)
        return value

    one, two = (total(first), total(second))
    piece[:, : 2 * ug] = one.astype(BF)
    piece[:, 2 * ug :] = two.astype(BF)
    one = muon_momentum * mom[:, : 2 * ug] + one
    two = muon_momentum * mom[:, 2 * ug :] + two
    slots[...] = jnp.zeros_like(slots)
    slots[0] = one[:, :ug].astype(BF)
    slots[1] = one[:, ug:].astype(BF)
    slots[2, :, :qg] = two[:, :qg].astype(BF)
    slots[3, :, : two.shape[1] - qg] = two[:, qg:].astype(BF)
    for step in range(group_count):
        outs[step][...] = slots[zone ^ step]


def split(value):
    high = value.astype(BF)
    return (high, (value - high.astype(F32)).astype(BF))


def dot32(left, right):
    return jnp.dot(left, right, preferred_element_type=F32)


def triple(left, right):
    return dot32(left[0], right[0]) + (dot32(left[0], right[1]) + dot32(left[1], right[0]))


def newton_kernel(count, place, *refs):
    parts, outs = (refs[:count], refs[count:-3])
    whole, gram, lead = refs[-3:]
    piece = parts[0].shape[0]
    for step, item in enumerate(parts):
        whole[step * piece : (step + 1) * piece, :] = item[...]
    matrix = whole[...]
    raw = lax.dot_general(matrix, matrix, (((1,), (1,)), ((), ())), preferred_element_type=F32)
    row = lax.broadcasted_iota(jnp.int32, raw.shape, 0)
    column = lax.broadcasted_iota(jnp.int32, raw.shape, 1)
    norm = jnp.sqrt(jnp.sum(jnp.where(row == column, raw, 0.0), keepdims=True))
    scale = 1.0 / (norm + frob_eps)
    gram[...] = raw * (scale * scale)
    lead[...] = jnp.where(row[:piece] == column[:piece], scale, 0.0)

    def sweep(index, carry):
        now = gram[...]
        pair = split(now)
        square = triple(pair, pair)
        poly = newton_second * now + newton_third * square
        front = lead[...]
        turn = split(poly)
        lead[...] = newton_first * front + triple(split(front), turn)
        mixed = newton_first * now + triple(turn, pair)
        gram[...] = newton_first * mixed + triple(turn, split(mixed))
        return carry

    lax.fori_loop(0, NS_STEPS - 1, sweep, 0)
    pair = split(gram[...])
    front = lead[...]
    once = triple(split(front), pair)
    twice = newton_second * front + newton_third * once
    front = newton_first * front + triple(split(twice), pair)
    high, low = split(front)
    width = outs[0].shape[1]
    for step, out in enumerate(outs):
        block = whole[:, step * width : (step + 1) * width]
        out[...] = (dot32(high, block) + dot32(low, block)).astype(BF)


def pack_kernel(group_count, qg, place, *refs):
    zone = place[2]
    out, stack = refs[group_count:]
    ug = stack.shape[2]
    for step in range(group_count):
        stack[step] = refs[step][...]
    out[:, :ug] = stack[zone]
    out[:, ug : 2 * ug] = stack[zone ^ 1]
    out[:, 2 * ug : 2 * ug + qg] = stack[zone ^ 2][:, :qg]
    out[:, 2 * ug + qg :] = stack[zone ^ 3][:, : out.shape[1] - 2 * ug - qg]


def spread(place, parts, ref, span):
    core, chip = (place[0], place[1])
    piece = parts[0].shape[0]
    near = len(parts) // 2
    for step, part in enumerate(parts):
        seat = core if step < near else 1 - core
        ref[rows_at(seat * HALF + (chip ^ (step % near)) * piece, piece), :] = part[:, span].astype(
            F32
        )


def grad_kernel(count, place, *refs):
    parts = refs[:count]
    mq, mp, mu, md = refs[count : count + 4]
    gq, gp, gu, gd, nq, np_, nu, nd, flip = refs[count + 4 :]
    ug, qg = (gu.shape[1], gq.shape[1])
    spread(place, parts, gu, slice(0, ug))
    spread(place, parts, flip, slice(ug, 2 * ug))
    spread(place, parts, gq, slice(2 * ug, 2 * ug + qg))
    spread(place, parts, gp, slice(2 * ug + qg, None))
    gd[...] = flip[...].T
    nq[...] = muon_momentum * mq[...] + gq[...]
    np_[...] = muon_momentum * mp[...] + gp[...]
    nu[...] = muon_momentum * mu[...] + gu[...]
    nd[...] = muon_momentum * md[...] + gd[...]


def weight_kernel(count, place, *refs):
    parts = refs[:count]
    wq, wp, wu, wd = refs[count : count + 4]
    nq, np_, nu, nd, flip = refs[count + 4 :]
    ug, qg = (nu.shape[1], nq.shape[1])
    spread(place, parts, nu, slice(0, ug))
    spread(place, parts, flip, slice(ug, 2 * ug))
    spread(place, parts, nq, slice(2 * ug, 2 * ug + qg))
    spread(place, parts, np_, slice(2 * ug + qg, None))
    for new, old, factor in (
        (nq, wq, math.sqrt(3.0)),
        (np_, wp, 1.0),
        (nu, wu, math.sqrt(max(1.0, FF / D))),
    ):
        new[...] = old[...] - muon_rate * (factor * new[...] + muon_decay * old[...])
    nd[...] = wd[...] - muon_rate * (flip[...].T + muon_decay * wd[...])


CELL = 64
AREA = WIN * WIN
CELLS = (SIDE // WIN) ** 2
FOUR = 4


def flat(left, right):
    return lax.dot_general(left, right, (((1,), (1,)), ((), ())), preferred_element_type=F32)


def tall(left, right):
    return lax.dot_general(left, right, (((0,), (0,)), ((), ())), preferred_element_type=F32)


def segment_sum(value, ones):
    high, low = split(value)
    return dot32(high, ones) + dot32(low, ones)


def place_rows(source, target, index, scratch, order, factor=None):
    tokens = source.shape[1]
    scratch[...] = jnp.zeros_like(scratch)
    value = source[index]
    scratch[:tokens, :] = value if factor is None else (value.astype(F32) * factor).astype(BF)
    size = order.shape[0]
    moved = dot32(order[...], scratch[...])
    target[index * size : (index + 1) * size, :] = moved.astype(target.dtype)


def attend_kernel(
    head_width,
    place,
    images,
    wq,
    wp,
    vectors,
    bias,
    order,
    heads,
    ones,
    resid,
    qkv,
    mixed,
    probs,
    normed,
    scaled,
    inverse,
    scratch,
):
    slots = images.shape[0]
    size = CELLS * CELL
    scale = head_width ** (-0.5)
    for slot in range(slots):
        place_rows(images, resid, slot, scratch, order)
    shift = jnp.concatenate([vectors[2:3, :], jnp.zeros((1, D), F32), vectors[3:4, :]], 1)

    def project(slot, carry):
        rows = rows_at(slot * size, size)
        hat, back = standard(resid[rows, :])
        scaled[rows, :] = hat
        inverse[rows, :] = jnp.broadcast_to(back, (size, inverse.shape[1]))
        value = (hat * vectors[0:1, :] + vectors[1:2, :]).astype(BF)
        normed[rows, :] = value
        seen = lax.broadcasted_iota(jnp.int32, (size, 1), 0) % CELL < AREA
        full = dot32(value, wq[...]) + shift
        qkv[rows, :] = jnp.where(seen, full, 0.0).astype(BF)
        return carry

    lax.fori_loop(0, slots, project, 0)

    def window(cell, carry):
        rows = rows_at(cell * CELL, CELL)
        for part in range(D // 128):
            lanes = slice(part * 128, part * 128 + 128)
            wide = slice(part * 256, part * 256 + 256)
            query = qkv[rows, lanes]
            key = qkv[rows, D + part * 128 : D + part * 128 + 128]
            value = qkv[rows, 2 * D + part * 128 : 2 * D + part * 128 + 128]
            keys = jnp.concatenate([key] * FOUR, 0) * heads[...]
            values = jnp.concatenate([value] * FOUR, 0) * heads[...]
            scores = flat(query, keys) * scale + bias[cell % CELLS, :, wide]
            total = segment_sum(jnp.exp(scores), ones[...])
            chance = jnp.exp(scores - jnp.log(total))
            probs[rows, wide] = chance
            mixed[rows, lanes] = dot32(chance.astype(BF), values).astype(BF)
        return carry

    lax.fori_loop(0, slots * CELLS, window, 0)

    def finish(slot, carry):
        rows = rows_at(slot * size, size)
        resid[rows, :] = resid[rows, :] + dot32(mixed[rows, :], wp[...]) + vectors[4:5, :]
        return carry

    lax.fori_loop(0, slots, finish, 0)


def standard(value):
    centred = value - jnp.mean(value, -1, keepdims=True)
    back = lax.rsqrt(jnp.mean(centred * centred, -1, keepdims=True) + norm_eps)
    return (centred * back, back)


def hidden_kernel(
    ug,
    place,
    resid,
    grads,
    wu,
    wd,
    vectors,
    bias,
    order,
    output,
    keep,
    send,
    resid_back,
    sums,
    bias_grad,
    scratch,
    upstream,
    normed,
    turned,
    raised,
    total,
    back,
    hidden,
    slanted,
):
    slots, tokens = (grads.shape[0], grads.shape[1])
    size = order.shape[0]
    core, count = (place[0], place[4])
    for slot in range(slots):
        factor = jnp.where(slot < count, 1.0, 0.0)
        place_rows(grads, upstream, slot, scratch, order, factor)
    for slot in range(slots):
        rows = slice(slot * size, (slot + 1) * size)
        hat, _ = standard(resid[rows, :])
        normed[rows, :] = (hat * vectors[5:6, :] + vectors[6:7, :]).astype(BF)
    turned[...] = normed[...].T
    raised[...] = upstream[...].T
    total[...] = jnp.zeros_like(total)
    back[...] = jnp.zeros_like(back)
    blend = math.sqrt(2.0 / math.pi)
    near, away = (rows_at(core * HALF, HALF), rows_at((1 - core) * HALF, HALF))

    def chunk(index, carry):
        lanes = rows_at(index * ug, ug)
        gain = jnp.zeros((1, ug), F32)
        for slot in range(slots):
            rows = slice(slot * size, (slot + 1) * size)
            inner = dot32(normed[rows, :], wu[:, lanes]) + bias[:, lanes]
            cube = inner * inner
            tangent = jnp.tanh(blend * (inner + 0.044715 * inner * cube))
            hidden[rows, :] = (0.5 * inner * (1.0 + tangent)).astype(BF)
            slope = 0.5 * (1.0 + tangent) + 0.5 * inner * (1.0 - tangent * tangent) * blend * (
                1.0 + 3.0 * 0.044715 * cube
            )
            grad = dot32(upstream[rows, :], wd[:, lanes]) * slope
            gain = gain + jnp.sum(grad, 0, keepdims=True)
            slanted[rows, :] = grad.astype(BF)
        bias_grad[:, lanes] = gain
        total[...] += flat(hidden[...], wd[:, lanes])
        back[...] += flat(slanted[...], wu[:, lanes])
        first = rows_at(index * 2 * ug, ug)
        second = pl.ds(pl.multiple_of(index * 2 * ug + ug, ug), ug)
        keep[:, first] = dot32(turned[near, :], slanted[...]).astype(BF)
        send[:, first] = dot32(turned[away, :], slanted[...]).astype(BF)
        keep[:, second] = dot32(raised[near, :], hidden[...]).astype(BF)
        send[:, second] = dot32(raised[away, :], hidden[...]).astype(BF)
        return carry

    lax.fori_loop(0, wu.shape[1] // ug, chunk, 0)
    sums[...] = jnp.zeros_like(sums)
    for slot in range(slots):
        rows = slice(slot * size, (slot + 1) * size)
        final = resid[rows, :] + total[rows, :] + vectors[7:8, :]
        final = (final * jnp.where(slot < count, 1.0, 0.0)).astype(BF)
        output[slot] = tall(order[...], final)[:tokens, :].astype(BF)
        hat, inverse = standard(resid[rows, :])
        given = upstream[rows, :].astype(F32)
        value = back[rows, :]
        result = given + norm_back(value * vectors[5:6, :], hat, inverse)
        resid_back[rows, :] = result
        sums[0:1, :] += jnp.sum(result, 0, keepdims=True)
        sums[1:2, :] += jnp.sum(value * hat, 0, keepdims=True)
        sums[2:3, :] += jnp.sum(value, 0, keepdims=True)
        sums[3:4, :] += jnp.sum(given, 0, keepdims=True)


def scatter_columns(ref, value, groups, offset, width):
    stride = ref.shape[1] // groups
    for group in range(groups):
        start = group * stride + offset
        ref[:, start : start + width] = value[:, group * width : (group + 1) * width]


def scores_kernel(
    head_width,
    groups,
    place,
    resid_back,
    wp,
    qkv,
    mixed,
    probs,
    normed,
    heads,
    ones,
    keep,
    send,
    grads,
    sums,
    table,
    rounded,
    mixed_back,
    turned,
):
    core = place[0]
    near, away = (rows_at(core * HALF, HALF), rows_at((1 - core) * HALF, HALF))
    scale = head_width ** (-0.5)
    cells = qkv.shape[0] // CELL
    qg = 3 * D // groups
    rounded[...] = resid_back[...].astype(BF)
    mixed_back[...] = flat(rounded[...], wp[...]).astype(BF)
    turned[...] = mixed[...].T
    for out, half in ((keep, near), (send, away)):
        value = dot32(turned[half, :], rounded[...]).astype(BF)
        scatter_columns(out, value, groups, qg, D // groups)
    table[...] = jnp.zeros_like(table)
    sums[...] = jnp.zeros_like(sums)

    def window(cell, carry):
        rows = rows_at(cell * CELL, CELL)
        for part in range(D // 128):
            lanes = slice(part * 128, part * 128 + 128)
            wide = slice(part * 256, part * 256 + 256)
            query = qkv[rows, lanes]
            key = qkv[rows, D + part * 128 : D + part * 128 + 128]
            value = qkv[rows, 2 * D + part * 128 : 2 * D + part * 128 + 128]
            given = mixed_back[rows, lanes]
            mask = heads[...]
            keys = jnp.concatenate([key] * FOUR, 0) * mask
            values = jnp.concatenate([value] * FOUR, 0) * mask
            chance = probs[rows, wide]
            prob_back = flat(given, values)
            level = segment_sum(chance * prob_back, ones[...])
            score = chance * (prob_back - level)
            table[:, wide] += score
            score = score.astype(BF)
            query_back = dot32(score, keys) * scale
            loose = mask.astype(F32)

            def fold(value):
                value = value * loose
                parts = [value[item * CELL : (item + 1) * CELL, :] for item in range(FOUR)]
                return (parts[0] + parts[1]) + (parts[2] + parts[3])

            key_back = fold(tall(score, query)) * scale
            value_back = fold(tall(chance.astype(BF), given))
            sums[0:1, lanes] += jnp.sum(query_back, 0, keepdims=True)
            sums[1:2, lanes] += jnp.sum(value_back, 0, keepdims=True)
            grads[rows, lanes] = query_back.astype(BF)
            grads[rows, D + part * 128 : D + part * 128 + 128] = key_back.astype(BF)
            grads[rows, 2 * D + part * 128 : 2 * D + part * 128 + 128] = value_back.astype(BF)
        return carry

    lax.fori_loop(0, cells, window, 0)
    turned[...] = normed[...].T
    for out, half in ((keep, near), (send, away)):
        value = dot32(turned[half, :], grads[...]).astype(BF)
        scatter_columns(out, value, groups, 0, qg)


def input_kernel(
    place, resid_back, grads, wq, scaled, inverse, vectors, order, input_grad, sums
):
    slots, tokens = (input_grad.shape[0], input_grad.shape[1])
    size = order.shape[0]
    sums[...] = jnp.zeros_like(sums)
    for slot in range(slots):
        rows = slice(slot * size, (slot + 1) * size)
        value = flat(grads[rows, :], wq[...])
        hat = scaled[rows, :]
        sums[0:1, :] += jnp.sum(value * hat, 0, keepdims=True)
        sums[1:2, :] += jnp.sum(value, 0, keepdims=True)
        result = resid_back[rows, :] + norm_back(
            value * vectors[0:1, :], hat, inverse[rows, 0:1]
        )
        high, low = split(result)
        moved = tall(order[...], high) + tall(order[...], low)
        input_grad[slot] = moved[:tokens, :]


def block_tables(heads):
    line = np.arange(SIDE)
    rolled = (line - SHIFT) % SIDE
    row, column = (np.repeat(rolled, SIDE), np.tile(rolled, SIDE))
    cell = (row // WIN) * (SIDE // WIN) + column // WIN
    spot = cell * CELL + (row % WIN) * WIN + column % WIN
    order = np.zeros((CELLS * CELL, CELLS * CELL), np.float32)
    order[spot, np.arange(SIDE * SIDE)] = 1.0
    masks = np.repeat(np.arange(FOUR), CELL)[:, None] == np.arange(128)[None, :] // (D // heads)
    spans = np.arange(FOUR * CELL) // CELL
    ones = spans[:, None] == spans[None, :]
    return tuple((jnp.asarray(item, BF) for item in (order, masks, ones)))


def position_tables(rel_table, onehot, blocked):
    heads = rel_table.shape[1]
    bias = jnp.dot(onehot, rel_table, precision=lax.Precision.HIGHEST)
    bias = bias.reshape(AREA, AREA, heads).transpose(0, 2, 1)[None] + blocked[:, :, None, :]
    bias = jnp.pad(bias, ((0, 0), (0, 0), (0, 0), (0, CELL - AREA)), constant_values=-1e30)
    bias = jnp.pad(bias, ((0, 0), (0, CELL - AREA), (0, 0), (0, 0)))
    inside = np.arange(CELL) < AREA
    edge = np.where(inside[:, None] | inside[None, :], 0.0, -1e30).astype(np.float32)
    bias = bias + jnp.asarray(edge)[None, :, None, :]
    return bias.reshape(CELLS, CELL, heads * CELL)


def table_sums(summed, onehot, heads):
    summed = summed.reshape(CELL, heads, CELL)[:AREA, :, :AREA].transpose(1, 0, 2)
    return jnp.dot(
        summed.reshape(heads, AREA * AREA), onehot, precision=lax.Precision.HIGHEST
    ).T


def adam(grad, param, first, second):
    first_new = beta_first * first + (1.0 - beta_first) * grad
    second_new = beta_second * second + (1.0 - beta_second) * grad * grad
    first_hat = first_new / (1.0 - beta_first**adam_count)
    second_hat = second_new / (1.0 - beta_second**adam_count)
    return (
        param - adam_rate * first_hat / (jnp.sqrt(second_hat) + adam_eps),
        first_new,
        second_new,
    )


def local(
    images,
    grad_output,
    live_count,
    qkv_weight,
    proj_weight,
    up_weight,
    down_weight,
    qkv_moment,
    proj_moment,
    up_moment,
    down_moment,
    vectors,
    hidden_bias,
    rel_table,
    vector_first,
    vector_second,
    bias_first,
    bias_second,
    table_first,
    table_second,
):
    onehot, blocked = window_tables(SIDE, WIN, SHIFT)
    groups, members = (lax.axis_size("group"), lax.axis_size("dp"))
    chips = members // 2
    piece = D // members
    seat, zone = (lax.axis_index("dp"), lax.axis_index("group"))
    place = jnp.stack([seat & 1, seat >> 1, zone, seat, live_count.reshape(())]).astype(jnp.int32)
    ug, qg, pg = (up_weight.shape[1], qkv_weight.shape[1], proj_weight.shape[1])

    def zshift(value, step):
        return lax.ppermute(value, "group", [(item, item ^ step) for item in range(groups)])

    def dshift(value, step):
        return lax.ppermute(value, "dp", [(item, item ^ step) for item in range(members)])

    shard_up, shard_qkv, part_up, part_qkv, moment_rows = run(
        prep_kernel,
        "prep",
        place,
        [
            qkv_weight,
            proj_weight,
            up_weight,
            down_weight,
            qkv_moment,
            proj_moment,
            up_moment,
            down_moment,
        ],
        [
            shape((D, 2 * ug), BF),
            shape((D, qg + pg), BF),
            shape((2 * PART, 2 * ug), BF),
            shape((2 * PART, qg + pg), BF),
            shape((piece, 2 * ug + qg + pg), F32),
        ],
        [pltpu.VMEM((D, ug), F32)],
    )

    def gather(shard, part, widths, name):
        far = [zshift(part, step) for step in range(1, groups)]
        across = dshift(jnp.concatenate([item[:PART] for item in far]), 2)
        along = dshift(jnp.concatenate([item[PART:] for item in far]), 4)
        mine = far + [across, along]
        theirs = [dshift(item, 1) for item in mine]
        fits = all((width % 128 == 0 for width in widths))
        kept = widths if fits else (sum(widths),)
        joined = run(
            functools.partial(join_kernel, groups, kept),
            name,
            place,
            [shard, *mine, *theirs],
            [shape((D, groups * width), BF) for width in kept],
        )
        if fits:
            return joined
        joined = joined[0].reshape(D, groups, -1)
        cut = widths[0]
        return [joined[:, :, :cut].reshape(D, -1), joined[:, :, cut:].reshape(D, -1)]

    full_qkv, full_proj = gather(shard_qkv, part_qkv, (qg, pg), "join_qkv")
    full_up, full_flip = gather(shard_up, part_up, (ug, ug), "join_up")
    heads = rel_table.shape[1]
    slots, tokens, _ = images.shape
    order, head_mask, ones = block_tables(heads)
    bias = position_tables(rel_table, onehot, blocked)
    size = CELLS * CELL
    rows = slots * size
    resid, qkv_rows, mixed, probs, normed, scaled, inverse = run(
        functools.partial(attend_kernel, D // heads),
        "attend",
        place,
        [images, full_qkv, full_proj, vectors, bias, order, head_mask, ones],
        [
            shape((rows, D), F32),
            shape((rows, 3 * D), BF),
            shape((rows, D), BF),
            shape((rows, heads * CELL), F32),
            shape((rows, D), BF),
            shape((rows, D), F32),
            shape((rows, 128), F32),
        ],
        [pltpu.VMEM((size, D), BF)],
    )
    output, keep_up, send_up, resid_back, sums_hidden, bias_sum = run(
        functools.partial(hidden_kernel, ug),
        "hidden",
        place,
        [resid, grad_output, full_up, full_flip, vectors, hidden_bias[None], order],
        [
            shape(images.shape, BF),
            shape((HALF, 2 * FF), BF),
            shape((HALF, 2 * FF), BF),
            shape((rows, D), F32),
            shape((4, D), F32),
            shape((1, FF), F32),
        ],
        [
            pltpu.VMEM((size, D), BF),
            pltpu.VMEM((rows, D), BF),
            pltpu.VMEM((rows, D), BF),
            pltpu.VMEM((D, rows), BF),
            pltpu.VMEM((D, rows), BF),
            pltpu.VMEM((rows, D), F32),
            pltpu.VMEM((rows, D), F32),
            pltpu.VMEM((rows, ug), BF),
            pltpu.VMEM((rows, ug), BF),
        ],
    )
    keep_qkv, send_qkv, qkv_back, sums_scores, table = run(
        functools.partial(scores_kernel, D // heads, groups),
        "scores",
        place,
        [resid_back, full_proj, qkv_rows, mixed, probs, normed, head_mask, ones],
        [
            shape((HALF, 4 * D), BF),
            shape((HALF, 4 * D), BF),
            shape((rows, 3 * D), BF),
            shape((2, D), F32),
            shape((CELL, heads * CELL), F32),
        ],
        [pltpu.VMEM((rows, D), BF), pltpu.VMEM((rows, D), BF), pltpu.VMEM((D, rows), BF)],
    )
    input_grad, sums_input = run(
        input_kernel,
        "inputs",
        place,
        [resid_back, qkv_back, full_qkv, scaled, inverse, vectors, order],
        [shape(images.shape, F32), shape((2, D), F32)],
    )
    local_vector = jnp.concatenate([sums_input, sums_scores, sums_hidden])
    local_bias = bias_sum[0]
    local_table = table_sums(table, onehot, heads)

    def reduce(keep, send, name):
        width = keep.shape[1]
        own, *sends = run(
            halve_kernel,
            "halve_" + name,
            place,
            [keep, dshift(send, 1)],
            [shape((piece, width), F32)] + [shape((piece, width), BF)] * (chips - 1),
        )
        came = [dshift(item, 2 * (step + 1)) for step, item in enumerate(sends)]
        width = width // groups
        own, *sends = run(
            functools.partial(plane_kernel, chips),
            "plane_" + name,
            place,
            [own, *came],
            [shape((piece, width), F32)] + [shape((piece, width), BF)] * (groups - 1),
        )
        return [own] + [zshift(item, step + 1) for step, item in enumerate(sends)]

    first = reduce(keep_up, send_up, "up")
    second = reduce(keep_qkv, send_qkv, "qkv")
    grad_piece, *outgoing = run(
        functools.partial(momentum_kernel, groups, qg),
        "momentum",
        place,
        [*first, *second, moment_rows],
        [shape((piece, 2 * ug + qg + pg), BF)] + [shape((piece, ug), BF)] * groups,
        [pltpu.VMEM((max(groups, 4), piece, ug), BF)],
    )

    def share(value):
        near = [value] + [dshift(value, 2 * step) for step in range(1, chips)]
        return near + [dshift(item, 1) for item in near]

    owned = [outgoing[0]] + [zshift(outgoing[step], step) for step in range(1, groups)]
    everyone = share(jnp.concatenate(owned, 1))
    results = run(
        functools.partial(newton_kernel, members),
        "newton",
        place,
        everyone,
        [shape((piece, ug), BF)] * groups,
        [
            pltpu.VMEM((D, groups * ug), BF),
            pltpu.VMEM((D, D), F32),
            pltpu.VMEM((piece, D), F32),
        ],
    )
    back = [results[0]] + [zshift(results[step], step) for step in range(1, groups)]
    (packed,) = run(
        functools.partial(pack_kernel, groups, qg),
        "pack",
        place,
        back,
        [shape((piece, 2 * ug + qg + pg), BF)],
        [pltpu.VMEM((groups, piece, ug), BF)],
    )
    mats = [(D, qg), (D, pg), (D, ug), (ug, D)]
    (
        qkv_grad,
        proj_grad,
        up_grad,
        down_grad,
        qkv_momentum,
        proj_momentum,
        up_momentum,
        down_momentum,
    ) = run(
        functools.partial(grad_kernel, members),
        "grads",
        place,
        [*share(grad_piece), qkv_moment, proj_moment, up_moment, down_moment],
        [shape(item, F32) for item in mats + mats],
        [pltpu.VMEM((D, ug), F32)],
    )
    new_qkv, new_proj, new_up, new_down = run(
        functools.partial(weight_kernel, members),
        "weights",
        place,
        [*share(packed), qkv_weight, proj_weight, up_weight, down_weight],
        [shape(item, F32) for item in mats],
        [pltpu.VMEM((D, ug), F32)],
    )
    small = jnp.concatenate(
        [local_vector.reshape(-1), local_bias.reshape(-1), local_table.reshape(-1)]
    )
    pad = -small.size % 1024
    total = jnp.pad(small, (0, pad)).reshape(-1, 128)
    step = 1
    while step < members:
        total = total + dshift(total, step)
        step *= 2
    step = 1
    while step < groups:
        total = total + zshift(total, step)
        step *= 2
    total = total.reshape(-1)
    ends = np.cumsum([local_vector.size, local_bias.size, local_table.size])
    vector_grad = total[: ends[0]].reshape(local_vector.shape)
    bias_grad = total[ends[0] : ends[1]].reshape(local_bias.shape)
    table_grad = total[ends[1] : ends[2]].reshape(local_table.shape)
    new_vectors, vector_mean, vector_square = adam(
        vector_grad, vectors, vector_first, vector_second
    )
    new_bias, bias_mean, bias_square = adam(bias_grad, hidden_bias, bias_first, bias_second)
    new_table, table_mean, table_square = adam(table_grad, rel_table, table_first, table_second)
    return (
        output,
        input_grad,
        qkv_grad,
        proj_grad,
        up_grad,
        down_grad,
        vector_grad,
        bias_grad,
        table_grad,
        new_qkv,
        new_proj,
        new_up,
        new_down,
        qkv_momentum,
        proj_momentum,
        up_momentum,
        down_momentum,
        new_vectors,
        new_bias,
        new_table,
        vector_mean,
        vector_square,
        bias_mean,
        bias_square,
        table_mean,
        table_square,
    )


def solution(mesh):
    placed = (
        P(("dp", "group"), None, None),
        P(("dp", "group"), None, None),
        P("dp", "group"),
        P(None, "group"),
        P(None, "group"),
        P(None, "group"),
        P("group", None),
        P(None, "group"),
        P(None, "group"),
        P(None, "group"),
        P("group", None),
        P(),
        P(),
        P(),
        P(),
        P(),
        P(),
        P(),
        P(),
        P(),
    )
    return jax.shard_map(
        local,
        mesh=mesh,
        in_specs=placed,
        out_specs=(
            P(("dp", "group"), None, None),
            P(("dp", "group"), None, None),
            P(None, "group"),
            P(None, "group"),
            P(None, "group"),
            P("group", None),
            P(),
            P(),
            P(),
            P(None, "group"),
            P(None, "group"),
            P(None, "group"),
            P("group", None),
            P(None, "group"),
            P(None, "group"),
            P(None, "group"),
            P("group", None),
            P(),
            P(),
            P(),
            P(),
            P(),
            P(),
            P(),
            P(),
            P(),
        ),
        check_vma=False,
    )
```

```python
import functools
import math

import jax
import jax.numpy as jnp
import numpy as np
from jax import lax
from jax.experimental import pallas as pl
from jax.experimental.pallas import tpu as pltpu
from jax.sharding import PartitionSpec as P

D = 512
FF = 2048
SIDE = 14
WIN = 7
SHIFT = 3
NS_STEPS = 5


norm_eps = 1e-05
mask_fill = -100.0
muon_momentum = 0.95
muon_rate = 0.4
muon_decay = 0.1
adam_rate = 0.1
beta_first = 0.9
beta_second = 0.999
adam_eps = 1e-08
adam_count = 10.0
frob_eps = 1e-06
newton_first = 3.4445
newton_second = -4.775
newton_third = 2.0315


def blocked_pairs(side, window, shift):
    line = np.arange(side)
    label = (line >= side - window).astype(np.int64) + (line >= side - shift).astype(np.int64)
    region = 3 * label[:, None] + label[None, :]
    per_side = side // window
    region = (
        region.reshape(per_side, window, per_side, window)
        .transpose(0, 2, 1, 3)
        .reshape(per_side * per_side, window * window)
    )
    return np.where(region[:, :, None] != region[:, None, :], mask_fill, 0.0).astype(np.float32)


def adam(grad, param, first, second):
    first_new = beta_first * first + (1.0 - beta_first) * grad
    second_new = beta_second * second + (1.0 - beta_second) * grad * grad
    first_hat = first_new / (1.0 - beta_first**adam_count)
    second_hat = second_new / (1.0 - beta_second**adam_count)
    return (
        param - adam_rate * first_hat / (jnp.sqrt(second_hat) + adam_eps),
        first_new,
        second_new,
    )


def norm_back(grad_scaled, scaled, inverse):
    centre = jnp.mean(grad_scaled, -1, keepdims=True)
    along = jnp.mean(grad_scaled * scaled, -1, keepdims=True)
    return inverse * (grad_scaled - centre - scaled * along)


BF = jnp.bfloat16
F32 = jnp.float32
HALF = D // 2
PART = D // 8


def shape(dims, kind):
    return jax.ShapeDtypeStruct(tuple(dims), kind)


def run(
    kernel, name, place, args, outs, scratch=(), far=(), raw=(), sent=(), room=4
):
    far = tuple(far)
    arrays = [*args, *outs]
    moved = sum((int(np.prod(item.shape)) * item.dtype.itemsize for item in arrays))
    held = sum(
        (
            int(np.prod(item.shape)) * jnp.dtype(item.dtype).itemsize
            for item in scratch
            if item.memory_space == pltpu.VMEM
        )
    )
    vmem = pl.BlockSpec(memory_space=pltpu.VMEM)
    hbm = pl.BlockSpec(memory_space=pltpu.HBM)
    buffers = [pltpu.VMEM(args[item].shape, args[item].dtype) for item in far]
    if far:
        buffers.append(pltpu.SemaphoreType.DMA((len(far),)))

    def body(seat, *refs):
        ins, rest = (list(refs[: len(args)]), list(refs[len(args) :]))
        if far:
            local, rest = (rest[len(outs) : len(outs) + len(far) + 1], rest)
            rest = rest[: len(outs)] + rest[len(outs) + len(far) + 1 :]
            copies = [
                pltpu.make_async_copy(ins[item], local[spot], local[-1].at[spot])
                for spot, item in enumerate(far)
            ]
            for copy in copies:
                copy.start()
            for copy in copies:
                copy.wait()
            for spot, item in enumerate(far):
                ins[item] = local[spot]
        kernel(seat, *ins, *rest)

    remote = set(far) | set(raw)
    return pl.pallas_call(
        body,
        out_shape=list(outs),
        in_specs=[pl.BlockSpec(memory_space=pltpu.SMEM)]
        + [hbm if item in remote else vmem for item in range(len(args))],
        out_specs=[hbm if item in sent else vmem for item in range(len(outs))],
        scratch_shapes=buffers + list(scratch),
        name=name,
        cost_estimate=pl.CostEstimate(flops=0, bytes_accessed=moved, transcendentals=0),
        compiler_params=pltpu.CompilerParams(
            vmem_limit_bytes=min(62 << 20, moved + held + (room << 20))
        ),
    )(place, *args)


def after(value, *others):
    return lax.optimization_barrier((value, *others))[0]


def rows_at(start, size):
    return pl.ds(pl.multiple_of(start, size), size)


def cast_kernel(place, left, right, shard, part):
    width = left.shape[1]
    shard[:, :width] = left[...].astype(BF)
    shard[:, width:] = right[...].astype(BF)
    part[...] = shard[rows_at(place[0] * HALF + (place[1] & 3) * PART, PART), :]


def turn_kernel(place, wu, wd, mq, mp, mu, md, shard, part, mom, flip):
    ug, qg = (wu.shape[1], mq.shape[1])
    shard[:, :ug] = wu[...].astype(BF)
    shard[:, ug:] = wd[...].T.astype(BF)
    part[...] = shard[rows_at(place[0] * HALF + (place[1] & 3) * PART, PART), :]
    flip[...] = md[...].T
    piece = mom.shape[0]
    source = rows_at(place[0] * HALF + place[1] * piece, piece)
    mom[:, :ug] = mu[source, :]
    mom[:, ug : 2 * ug] = flip[source, :]
    mom[:, 2 * ug : 2 * ug + qg] = mq[source, :]
    mom[:, 2 * ug + qg :] = mp[source, :]


def join_kernel(group_count, widths, place, own, *refs):
    core, chip, zone = (place[0], place[1] & 3, place[2])
    parts, outs = (refs[:8], refs[8:])
    offset = 0
    for out, width in zip(outs, widths):
        span = slice(offset, offset + width)
        out[:, rows_at(zone * width, width)] = own[:, span]
        for step in range(1, group_count):
            columns = rows_at((zone ^ step) * width, width)
            for index, part in enumerate(parts):
                seat = core if index < 4 else 1 - core
                rows = rows_at(seat * HALF + (chip ^ (index % 4)) * PART, PART)
                out[rows, columns] = part[(step - 1) * PART : step * PART, span]
        offset += width


def stack_kernel(axis, place, *refs):
    parts, out, sems = (refs[:-2], refs[-2], refs[-1])
    size = parts[0].shape[axis]
    copies = []
    for step, part in enumerate(parts):
        span = pl.ds(step * size, size)
        target = out.at[span, :] if axis == 0 else out.at[:, span]
        copies.append(pltpu.make_async_copy(part, target, sems.at[step]))
    for copy in copies:
        copy.start()
    for copy in copies:
        copy.wait()


def weight_copies(place, groups, widths, sources, targets, sems):
    if len(sources) == len(targets):
        return [
            [pltpu.make_async_copy(source, target, sems.at[spot])]
            for spot, (source, target) in enumerate(zip(sources, targets))
        ]
    core, chip, zone = (place[0], place[1] & 3, place[2])
    own, parts = (sources[0], sources[1:])
    result, offset, spot = ([], 0, 0)
    for target, width in zip(targets, widths):
        span = pl.ds(offset, width)
        copies = [
            pltpu.make_async_copy(
                own.at[:, span], target.at[:, rows_at(zone * width, width)], sems.at[spot]
            )
        ]
        spot += 1
        for step in range(1, groups):
            columns = rows_at((zone ^ step) * width, width)
            for index, part in enumerate(parts):
                seat = core if index < 4 else 1 - core
                rows = rows_at(seat * HALF + (chip ^ (index % 4)) * PART, PART)
                source = part.at[pl.ds((step - 1) * PART, PART), span]
                copies.append(
                    pltpu.make_async_copy(source, target.at[rows, columns], sems.at[spot])
                )
                spot += 1
        result.append(copies)
        offset += width
    return result


def add_kernel(place, left, right, out):
    out[...] = left[...] + right[...]


def halve_kernel(place, keep, came, own, *sends):
    chip = place[1]
    piece = own.shape[0]

    def total(step):
        source = rows_at((chip ^ step) * piece, piece)
        return keep[source, :].astype(F32) + came[source, :].astype(F32)

    own[...] = total(0)
    for step, send in enumerate(sends):
        send[...] = total(step + 1).astype(BF)


def plane_kernel(chips, place, *refs):
    zone = place[2]
    own, came, outs = (refs[0], refs[1:chips], refs[chips:])
    width = outs[0].shape[1]

    def total(step):
        columns = rows_at((zone ^ step) * width, width)
        value = own[:, columns]
        for item in came:
            value = value + item[:, columns].astype(F32)
        return value

    outs[0][...] = total(0)
    for step in range(1, len(outs)):
        outs[step][...] = total(step).astype(BF)


def momentum_kernel(group_count, qg, place, *refs):
    zone = place[2]
    first = refs[:group_count]
    second = refs[group_count : 2 * group_count]
    mom, piece = refs[2 * group_count : 2 * group_count + 2]
    outs, slots = (refs[2 * group_count + 2 : -1], refs[-1])
    ug = slots.shape[2]

    def total(parts):
        value = parts[0][...]
        for item in parts[1:]:
            value = value + item[...].astype(F32)
        return value

    one, two = (total(first), total(second))
    piece[:, : 2 * ug] = one.astype(BF)
    piece[:, 2 * ug :] = two.astype(BF)
    one = muon_momentum * mom[:, : 2 * ug] + one
    two = muon_momentum * mom[:, 2 * ug :] + two
    slots[...] = jnp.zeros_like(slots)
    slots[0] = one[:, :ug].astype(BF)
    slots[1] = one[:, ug:].astype(BF)
    slots[2, :, :qg] = two[:, :qg].astype(BF)
    slots[3, :, : two.shape[1] - qg] = two[:, qg:].astype(BF)
    for step in range(group_count):
        outs[step][...] = slots[zone ^ step]


def split(value):
    high = value.astype(BF)
    return (high, (value - high.astype(F32)).astype(BF))


def dot32(left, right):
    return jnp.dot(left, right, preferred_element_type=F32)


def triple(left, right):
    return dot32(left[0], right[0]) + (dot32(left[0], right[1]) + dot32(left[1], right[0]))


def newton_kernel(count, place, *refs):
    parts, outs = (refs[:count], refs[count:-4])
    whole, gram, lead, sems = refs[-4:]
    piece = parts[0].shape[0]
    copies = [
        pltpu.make_async_copy(item, whole.at[pl.ds(step * piece, piece), :], sems.at[step])
        for step, item in enumerate(parts)
    ]
    for copy in copies:
        copy.start()
    for copy in copies:
        copy.wait()
    matrix = whole[...]
    raw = lax.dot_general(matrix, matrix, (((1,), (1,)), ((), ())), preferred_element_type=F32)
    row = lax.broadcasted_iota(jnp.int32, raw.shape, 0)
    column = lax.broadcasted_iota(jnp.int32, raw.shape, 1)
    norm = jnp.sqrt(jnp.sum(jnp.where(row == column, raw, 0.0), keepdims=True))
    scale = 1.0 / (norm + frob_eps)
    gram[...] = raw * (scale * scale)
    lead[...] = jnp.where(row[:piece] == column[:piece], scale, 0.0)

    def sweep(index, carry):
        now = gram[...]
        pair = split(now)
        square = triple(pair, pair)
        poly = newton_second * now + newton_third * square
        front = lead[...]
        turn = split(poly)
        lead[...] = newton_first * front + triple(split(front), turn)
        mixed = newton_first * now + triple(turn, pair)
        gram[...] = newton_first * mixed + triple(turn, split(mixed))
        return carry

    lax.fori_loop(0, NS_STEPS - 1, sweep, 0)
    pair = split(gram[...])
    front = lead[...]
    once = triple(split(front), pair)
    twice = newton_second * front + newton_third * once
    front = newton_first * front + triple(split(twice), pair)
    high, low = split(front)
    width = outs[0].shape[1]
    for step, out in enumerate(outs):
        block = whole[:, step * width : (step + 1) * width]
        out[...] = (dot32(high, block) + dot32(low, block)).astype(BF)


def pack_kernel(group_count, qg, place, *refs):
    zone = place[2]
    out, stack = refs[group_count:]
    ug = stack.shape[2]
    for step in range(group_count):
        stack[step] = refs[step][...]
    out[:, :ug] = stack[zone]
    out[:, ug : 2 * ug] = stack[zone ^ 1]
    out[:, 2 * ug : 2 * ug + qg] = stack[zone ^ 2][:, :qg]
    out[:, 2 * ug + qg :] = stack[zone ^ 3][:, : out.shape[1] - 2 * ug - qg]


def spread(place, parts, ref, span):
    core, chip = (place[0], place[1])
    piece = parts[0].shape[0]
    near = len(parts) // 2
    for step, part in enumerate(parts):
        seat = core if step < near else 1 - core
        ref[rows_at(seat * HALF + (chip ^ (step % near)) * piece, piece), :] = part[:, span].astype(
            F32
        )


def load(sources, targets, sems):
    copies = [
        pltpu.make_async_copy(source, target, sems.at[spot])
        for spot, (source, target) in enumerate(zip(sources, targets))
    ]
    for copy in copies:
        copy.start()
    return copies


def spans_of(ug, qg, pg):
    return (
        slice(0, ug),
        slice(ug, 2 * ug),
        slice(2 * ug, 2 * ug + qg),
        slice(2 * ug + qg, 2 * ug + qg + pg),
    )


def grad_kernel(count, place, *refs):
    sources, outs = (refs[: count + 4], refs[count + 4 : count + 12])
    held, rest = (refs[count + 12 : 2 * count + 16], refs[2 * count + 16 :])
    grads, news, flip, sems, out_sems = (rest[:4], rest[4:8], rest[8], rest[9], rest[10])
    copies = load(sources, held, sems)
    parts, moments = (held[:count], held[count:])
    for copy in copies[:count]:
        copy.wait()
    ug, qg, pg = (moments[0].shape[1], moments[2].shape[1], moments[3].shape[1])
    waits = []
    for item, span in enumerate(spans_of(ug, qg, pg)):
        copies[count + item].wait()
        if item == 1:
            spread(place, parts, flip, span)
            grads[item][...] = flip[...].T
        else:
            spread(place, parts, grads[item], span)
        news[item][...] = muon_momentum * moments[item][...] + grads[item][...]
        for spot, source in ((2 * item, grads[item]), (2 * item + 1, news[item])):
            copy = pltpu.make_async_copy(source, outs[spot], out_sems.at[spot])
            copy.start()
            waits.append(copy)
    for copy in waits:
        copy.wait()


def weight_kernel(count, place, *refs):
    sources, outs = (refs[: count + 4], refs[count + 4 : count + 8])
    held, rest = (refs[count + 8 : 2 * count + 12], refs[2 * count + 12 :])
    news, flip, sems, out_sems = (rest[:4], rest[4], rest[5], rest[6])
    copies = load(sources, held, sems)
    parts, olds = (held[:count], held[count:])
    for copy in copies[:count]:
        copy.wait()
    ug, qg, pg = (olds[0].shape[1], olds[2].shape[1], olds[3].shape[1])
    factors = (math.sqrt(max(1.0, FF / D)), 1.0, math.sqrt(3.0), 1.0)
    waits = []
    for item, span in enumerate(spans_of(ug, qg, pg)):
        copies[count + item].wait()
        spread(place, parts, flip if item == 1 else news[item], span)
        ortho = flip[...].T if item == 1 else news[item][...]
        old = olds[item][...]
        news[item][...] = old - muon_rate * (factors[item] * ortho + muon_decay * old)
        copy = pltpu.make_async_copy(news[item], outs[item], out_sems.at[item])
        copy.start()
        waits.append(copy)
    for copy in waits:
        copy.wait()


def adam_kernel(place, left, right, *refs):
    total = left[...] + right[...]
    ins, outs = (refs[:9], refs[9:])
    heads, offsets = ins[6].shape
    grads = (
        total[:8, :],
        jnp.concatenate([total[8 + item : 9 + item, :] for item in range(FF // D)], 1),
        total[12 : 12 + heads, :offsets],
    )
    for item, grad in enumerate(grads):
        value, first, second = (ref[...] for ref in ins[3 * item : 3 * item + 3])
        updated = adam(grad, value, first, second)
        for out, result in zip(outs[4 * item : 4 * item + 4], (grad, *updated)):
            out[...] = result


CELL = 64
AREA = WIN * WIN
CELLS = (SIDE // WIN) ** 2
FOUR = 4


def flat(left, right):
    return lax.dot_general(left, right, (((1,), (1,)), ((), ())), preferred_element_type=F32)


def tall(left, right):
    return lax.dot_general(left, right, (((0,), (0,)), ((), ())), preferred_element_type=F32)


def segment_sum(value, ones):
    high, low = split(value)
    return dot32(high, ones) + dot32(low, ones)


def place_rows(source, target, index, scratch, order, factor=None):
    tokens = source.shape[1]
    scratch[...] = jnp.zeros_like(scratch)
    value = source[index]
    scratch[:tokens, :] = value if factor is None else (value.astype(F32) * factor).astype(BF)
    size = order.shape[0]
    moved = dot32(order[...], scratch[...])
    target[index * size : (index + 1) * size, :] = moved.astype(target.dtype)


def attend_kernel(head_width, groups, widths, count, place, images, vectors, bias, *refs):
    order, heads, ones = refs[:3]
    sources, rest = (refs[3 : 3 + count], refs[3 + count :])
    resid, qkv, mixed, probs, normed, scaled, inverse, wq, wp, scratch, sems = rest
    slots = images.shape[0]
    size = CELLS * CELL
    scale = head_width ** (-0.5)
    first, second = weight_copies(place, groups, widths, sources, (wq, wp), sems)
    for copy in first + second:
        copy.start()
    for slot in range(slots):
        place_rows(images, resid, slot, scratch, order)
    for copy in first:
        copy.wait()
    shift = jnp.concatenate([vectors[2:3, :], jnp.zeros((1, D), F32), vectors[3:4, :]], 1)

    def project(slot, carry):
        rows = rows_at(slot * size, size)
        hat, back = standard(resid[rows, :])
        scaled[rows, :] = hat
        inverse[rows, :] = jnp.broadcast_to(back, (size, inverse.shape[1]))
        value = (hat * vectors[0:1, :] + vectors[1:2, :]).astype(BF)
        normed[rows, :] = value
        seen = lax.broadcasted_iota(jnp.int32, (size, 1), 0) % CELL < AREA
        full = dot32(value, wq[...]) + shift
        qkv[rows, :] = jnp.where(seen, full, 0.0).astype(BF)
        return carry

    lax.fori_loop(0, slots, project, 0)

    def window(cell, carry):
        rows = rows_at(cell * CELL, CELL)
        for part in range(D // 128):
            lanes = slice(part * 128, part * 128 + 128)
            wide = slice(part * 256, part * 256 + 256)
            query = qkv[rows, lanes]
            key = qkv[rows, D + part * 128 : D + part * 128 + 128]
            value = qkv[rows, 2 * D + part * 128 : 2 * D + part * 128 + 128]
            keys = jnp.concatenate([key] * FOUR, 0) * heads[...]
            values = jnp.concatenate([value] * FOUR, 0) * heads[...]
            scores = flat(query, keys) * scale + bias[cell % CELLS, :, wide]
            total = segment_sum(jnp.exp(scores), ones[...])
            chance = jnp.exp(scores - jnp.log(total))
            probs[rows, wide] = chance
            mixed[rows, lanes] = dot32(chance.astype(BF), values).astype(BF)
        return carry

    lax.fori_loop(0, slots * CELLS, window, 0)

    for copy in second:
        copy.wait()

    def finish(slot, carry):
        rows = rows_at(slot * size, size)
        resid[rows, :] = resid[rows, :] + dot32(mixed[rows, :], wp[...]) + vectors[4:5, :]
        return carry

    lax.fori_loop(0, slots, finish, 0)


def standard(value):
    centred = value - jnp.mean(value, -1, keepdims=True)
    back = lax.rsqrt(jnp.mean(centred * centred, -1, keepdims=True) + norm_eps)
    return (centred * back, back)


def hidden_kernel(ug, groups, count, place, resid, grads, vectors, bias, order, *refs):
    sources, rest = (refs[:count], refs[count:])
    output, keep, send, resid_back, sums, bias_grad = rest[:6]
    wu, wd, scratch, upstream, normed, turned, raised, total, back, hidden, slanted, sems = rest[6:]
    first, second = weight_copies(place, groups, (ug, ug), sources, (wu, wd), sems)
    for copy in first + second:
        copy.start()
    slots, tokens = (grads.shape[0], grads.shape[1])
    size = order.shape[0]
    core, count = (place[0], place[4])
    for slot in range(slots):
        factor = jnp.where(slot < count, 1.0, 0.0)
        place_rows(grads, upstream, slot, scratch, order, factor)
    for slot in range(slots):
        rows = slice(slot * size, (slot + 1) * size)
        hat, _ = standard(resid[rows, :])
        normed[rows, :] = (hat * vectors[5:6, :] + vectors[6:7, :]).astype(BF)
    turned[...] = normed[...].T
    raised[...] = upstream[...].T
    total[...] = jnp.zeros_like(total)
    back[...] = jnp.zeros_like(back)
    for copy in first + second:
        copy.wait()
    blend = math.sqrt(2.0 / math.pi)
    near, away = (rows_at(core * HALF, HALF), rows_at((1 - core) * HALF, HALF))

    def chunk(index, carry):
        lanes = rows_at(index * ug, ug)
        gain = jnp.zeros((1, ug), F32)
        for slot in range(slots):
            rows = slice(slot * size, (slot + 1) * size)
            inner = dot32(normed[rows, :], wu[:, lanes]) + bias[:, lanes]
            cube = inner * inner
            tangent = jnp.tanh(blend * (inner + 0.044715 * inner * cube))
            hidden[rows, :] = (0.5 * inner * (1.0 + tangent)).astype(BF)
            slope = 0.5 * (1.0 + tangent) + 0.5 * inner * (1.0 - tangent * tangent) * blend * (
                1.0 + 3.0 * 0.044715 * cube
            )
            grad = dot32(upstream[rows, :], wd[:, lanes]) * slope
            gain = gain + jnp.sum(grad, 0, keepdims=True)
            slanted[rows, :] = grad.astype(BF)
        bias_grad[:, lanes] = gain
        total[...] += flat(hidden[...], wd[:, lanes])
        back[...] += flat(slanted[...], wu[:, lanes])
        first = rows_at(index * 2 * ug, ug)
        second = pl.ds(pl.multiple_of(index * 2 * ug + ug, ug), ug)
        keep[:, first] = dot32(turned[near, :], slanted[...]).astype(BF)
        send[:, first] = dot32(turned[away, :], slanted[...]).astype(BF)
        keep[:, second] = dot32(raised[near, :], hidden[...]).astype(BF)
        send[:, second] = dot32(raised[away, :], hidden[...]).astype(BF)
        return carry

    lax.fori_loop(0, wu.shape[1] // ug, chunk, 0)
    sums[...] = jnp.zeros_like(sums)
    for slot in range(slots):
        rows = slice(slot * size, (slot + 1) * size)
        final = resid[rows, :] + total[rows, :] + vectors[7:8, :]
        final = (final * jnp.where(slot < count, 1.0, 0.0)).astype(BF)
        output[slot] = tall(order[...], final)[:tokens, :].astype(BF)
        hat, inverse = standard(resid[rows, :])
        given = upstream[rows, :].astype(F32)
        value = back[rows, :]
        result = given + norm_back(value * vectors[5:6, :], hat, inverse)
        resid_back[rows, :] = result
        sums[0:1, :] += jnp.sum(result, 0, keepdims=True)
        sums[1:2, :] += jnp.sum(value * hat, 0, keepdims=True)
        sums[2:3, :] += jnp.sum(value, 0, keepdims=True)
        sums[3:4, :] += jnp.sum(given, 0, keepdims=True)


def scatter_columns(ref, value, groups, offset, width):
    stride = ref.shape[1] // groups
    for group in range(groups):
        start = group * stride + offset
        ref[:, start : start + width] = value[:, group * width : (group + 1) * width]


def proj_kernel(place, resid_back, wp, mixed, keep, send, mixed_back, rounded, turned):
    core = place[0]
    rounded[...] = resid_back[...].astype(BF)
    mixed_back[...] = flat(rounded[...], wp[...]).astype(BF)
    turned[...] = mixed[...].T
    for out, half in ((keep, core), (send, 1 - core)):
        out[...] = dot32(turned[rows_at(half * HALF, HALF), :], rounded[...]).astype(BF)


def scores_kernel(
    head_width,
    groups,
    place,
    mixed_back,
    keep_proj,
    send_proj,
    qkv,
    probs,
    normed,
    heads,
    ones,
    keep,
    send,
    grads,
    sums,
    table,
    turned,
):
    core = place[0]
    near, away = (rows_at(core * HALF, HALF), rows_at((1 - core) * HALF, HALF))
    scale = head_width ** (-0.5)
    cells = qkv.shape[0] // CELL
    qg = 3 * D // groups
    for out, value in ((keep, keep_proj), (send, send_proj)):
        scatter_columns(out, value, groups, qg, D // groups)
    table[...] = jnp.zeros_like(table)
    sums[...] = jnp.zeros_like(sums)

    def window(cell, carry):
        rows = rows_at(cell * CELL, CELL)
        for part in range(D // 128):
            lanes = slice(part * 128, part * 128 + 128)
            wide = slice(part * 256, part * 256 + 256)
            query = qkv[rows, lanes]
            key = qkv[rows, D + part * 128 : D + part * 128 + 128]
            value = qkv[rows, 2 * D + part * 128 : 2 * D + part * 128 + 128]
            given = mixed_back[rows, lanes]
            mask = heads[...]
            keys = jnp.concatenate([key] * FOUR, 0) * mask
            values = jnp.concatenate([value] * FOUR, 0) * mask
            chance = probs[rows, wide]
            prob_back = flat(given, values)
            level = segment_sum(chance * prob_back, ones[...])
            score = chance * (prob_back - level)
            table[:, wide] += score
            score = score.astype(BF)
            query_back = dot32(score, keys) * scale
            loose = mask.astype(F32)

            def fold(value):
                value = value * loose
                parts = [value[item * CELL : (item + 1) * CELL, :] for item in range(FOUR)]
                return (parts[0] + parts[1]) + (parts[2] + parts[3])

            key_back = fold(tall(score, query)) * scale
            value_back = fold(tall(chance.astype(BF), given))
            sums[0:1, lanes] += jnp.sum(query_back, 0, keepdims=True)
            sums[1:2, lanes] += jnp.sum(value_back, 0, keepdims=True)
            grads[rows, lanes] = query_back.astype(BF)
            grads[rows, D + part * 128 : D + part * 128 + 128] = key_back.astype(BF)
            grads[rows, 2 * D + part * 128 : 2 * D + part * 128 + 128] = value_back.astype(BF)
        return carry

    lax.fori_loop(0, cells, window, 0)
    turned[...] = normed[...].T
    for out, half in ((keep, near), (send, away)):
        value = dot32(turned[half, :], grads[...]).astype(BF)
        scatter_columns(out, value, groups, 0, qg)


def input_kernel(place, *refs):
    resid_back, grads, wq, scaled, inverse, vectors, order, sums_scores, sums_hidden = refs[:9]
    bias_sum, table, spots, groups, input_grad, small, stack = refs[9:]
    slots, tokens = (input_grad.shape[0], input_grad.shape[1])
    size = order.shape[0]
    small[...] = jnp.zeros_like(small)
    for slot in range(slots):
        rows = slice(slot * size, (slot + 1) * size)
        value = flat(grads[rows, :], wq[...])
        hat = scaled[rows, :]
        small[0:1, :] += jnp.sum(value * hat, 0, keepdims=True)
        small[1:2, :] += jnp.sum(value, 0, keepdims=True)
        result = resid_back[rows, :] + norm_back(
            value * vectors[0:1, :], hat, inverse[rows, 0:1]
        )
        high, low = split(result)
        moved = tall(order[...], high) + tall(order[...], low)
        input_grad[slot] = moved[:tokens, :]
    small[2:4, :] = sums_scores[...]
    small[4:8, :] = sums_hidden[...]
    for item in range(FF // D):
        small[8 + item : 9 + item, :] = bias_sum[:, item * D : (item + 1) * D]
    heads = table.shape[1] // CELL
    for head in range(heads):
        stack[head * CELL : (head + 1) * CELL, :] = table[:, head * CELL : (head + 1) * CELL]
    for head in range(heads):
        high, low = split(stack[head * CELL : (head + 1) * CELL, :])
        spread_out = dot32(high, spots[...]) + dot32(low, spots[...])
        moved = pltpu.roll(spread_out, 0, 1, stride=1, stride_axis=0)
        high, low = split(moved)
        banded = dot32(groups[...], high) + dot32(groups[...], low)
        moved = pltpu.roll(banded, 0, 1, stride=WIN - 1, stride_axis=0)
        small[12 + head : 13 + head, : moved.shape[1]] = jnp.sum(moved, 0, keepdims=True)


def block_tables(heads):
    line = np.arange(SIDE)
    rolled = (line - SHIFT) % SIDE
    row, column = (np.repeat(rolled, SIDE), np.tile(rolled, SIDE))
    cell = (row // WIN) * (SIDE // WIN) + column // WIN
    spot = cell * CELL + (row % WIN) * WIN + column % WIN
    order = np.zeros((CELLS * CELL, CELLS * CELL), np.float32)
    order[spot, np.arange(SIDE * SIDE)] = 1.0
    masks = np.repeat(np.arange(FOUR), CELL)[:, None] == np.arange(128)[None, :] // (D // heads)
    spans = np.arange(FOUR * CELL) // CELL
    ones = spans[:, None] == spans[None, :]
    step = np.arange(AREA)
    spots = np.zeros((CELL, 256), np.float32)
    reach = 2 * WIN - 1
    spots[step, reach * (WIN - 1) + WIN - 1 - reach * (step // WIN) - step % WIN] = 1.0
    bands = np.zeros((8, CELL), np.float32)
    bands[step // WIN, step] = 1.0
    return tuple((jnp.asarray(item, BF) for item in (order, masks, ones, spots, bands)))


def exact(left, right):
    high = left.astype(BF)
    rest = left - high.astype(F32)
    middle = rest.astype(BF)
    low = (rest - middle.astype(F32)).astype(BF)
    return dot32(high, right) + (dot32(middle, right) + dot32(low, right))


def bias_kernel(place, table, reverse, bands, picks, masks, bias, padded):
    heads, offsets = table.shape
    padded[...] = jnp.zeros_like(padded)
    padded[:, :offsets] = table[...]
    turned = exact(padded[...], reverse[...])
    for pair in range(heads // 2):
        both = []
        for head in (2 * pair, 2 * pair + 1):
            line = jnp.broadcast_to(turned[head : head + 1, :], (8, turned.shape[1]))
            line = pltpu.roll(line, 0, 1, stride=WIN - 1, stride_axis=0)
            line = exact_left(bands[...], line)
            line = pltpu.roll(line, 0, 1, stride=1, stride_axis=0)
            both.append(exact(line, picks[...]))
        value = jnp.concatenate(both, 1)
        for cell in range(CELLS):
            bias[cell, :, pair * 128 : pair * 128 + 128] = value + masks[cell]


def exact_left(left, right):
    high = right.astype(BF)
    rest = right - high.astype(F32)
    middle = rest.astype(BF)
    low = (rest - middle.astype(F32)).astype(BF)
    return tall(left, high) + (tall(left, middle) + tall(left, low))


def position_tables(blocked):
    reach = 2 * WIN - 1
    step = np.arange(AREA)
    spot = reach * (step // WIN) + step % WIN
    reverse = np.zeros((256, 256), np.float32)
    line = np.arange(reach * reach)
    reverse[line, reach * reach - 1 - line] = 1.0
    picks = np.zeros((256, CELL), np.float32)
    picks[reach * (WIN - 1) + WIN - 1 + spot, step] = 1.0
    inside = np.arange(CELL) < AREA
    masks = np.zeros((CELLS, CELL, CELL), np.float32)
    masks[:, :AREA, :AREA] = blocked
    masks = masks + np.where(inside[None, :], 0.0, -1e30).astype(np.float32)
    masks = np.concatenate([masks, masks], 2)
    return (jnp.asarray(reverse, BF), jnp.asarray(picks, BF), jnp.asarray(masks))


def local(
    images,
    grad_output,
    live_count,
    qkv_weight,
    proj_weight,
    up_weight,
    down_weight,
    qkv_moment,
    proj_moment,
    up_moment,
    down_moment,
    vectors,
    hidden_bias,
    rel_table,
    vector_first,
    vector_second,
    bias_first,
    bias_second,
    table_first,
    table_second,
):
    groups, members = (lax.axis_size("group"), lax.axis_size("dp"))
    chips = members // 2
    piece = D // members
    seat, zone = (lax.axis_index("dp"), lax.axis_index("group"))
    place = jnp.stack([seat & 1, seat >> 1, zone, seat, live_count.reshape(())]).astype(jnp.int32)
    ug, qg, pg = (up_weight.shape[1], qkv_weight.shape[1], proj_weight.shape[1])

    def zshift(value, step):
        return lax.ppermute(value, "group", [(item, item ^ step) for item in range(groups)])

    def dshift(value, step):
        return lax.ppermute(value, "dp", [(item, item ^ step) for item in range(members)])

    shard_qkv, part_qkv = run(
        cast_kernel,
        "cast",
        place,
        [qkv_weight, proj_weight],
        [shape((D, qg + pg), BF), shape((PART, qg + pg), BF)],
        far=range(2),
        room=62,
    )
    shard_up, part_up, moment_rows = run(
        turn_kernel,
        "turn",
        after(place, part_qkv),
        [up_weight, down_weight, qkv_moment, proj_moment, up_moment, down_moment],
        [
            shape((D, 2 * ug), BF),
            shape((PART, 2 * ug), BF),
            shape((piece, 2 * ug + qg + pg), F32),
        ],
        [pltpu.VMEM((D, ug), F32)],
        far=range(6),
        room=62,
    )

    heads = rel_table.shape[1]
    order, head_mask, ones, spots, bands = block_tables(heads)
    reverse, picks, masks = position_tables(blocked_pairs(SIDE, WIN, SHIFT))
    (bias,) = run(
        bias_kernel,
        "bias",
        after(place, part_up),
        [rel_table.T, reverse, bands, picks, masks],
        [shape((CELLS, CELL, heads * CELL), F32)],
        [pltpu.VMEM((heads, 256), F32)],
        far=range(5),
    )

    def stack(parts, axis, name, order_by):
        dims = list(parts[0].shape)
        dims[axis] *= len(parts)
        (result,) = run(
            functools.partial(stack_kernel, axis),
            name,
            after(place, *order_by),
            parts,
            [shape(dims, BF)],
            [pltpu.SemaphoreType.DMA((len(parts),))],
            raw=range(len(parts)),
        )
        return result

    def fetch(part, name, *order_by):
        return stack([zshift(part, step) for step in range(1, groups)], 0, name, order_by)

    def gather(shard, far):
        mine = [far] + [dshift(far, 2 * step) for step in range(1, 4)]
        return [shard, *mine, *(dshift(item, 1) for item in mine)]

    far_qkv = fetch(part_qkv, "far_qkv", bias)
    far_up = fetch(after(part_up, far_qkv), "far_up")
    pieces_qkv = gather(shard_qkv, far_qkv)
    pieces_up = gather(shard_up, far_up)
    if qg % 128 or pg % 128:
        (joined,) = run(
            functools.partial(join_kernel, groups, (qg + pg,)),
            "join",
            place,
            pieces_qkv,
            [shape((D, groups * (qg + pg)), BF)],
        )
        joined = joined.reshape(D, groups, -1)
        pieces_qkv = [joined[:, :, :qg].reshape(D, -1), joined[:, :, qg:].reshape(D, -1)]
    slots, tokens, _ = images.shape
    size = CELLS * CELL
    rows = slots * size
    count = len(pieces_qkv)
    resid, qkv_rows, mixed, probs, normed, scaled, inverse, full_qkv, full_proj = run(
        functools.partial(attend_kernel, D // heads, groups, (qg, pg), count),
        "attend",
        after(place, far_up),
        [images, vectors, bias, order, head_mask, ones, *pieces_qkv],
        [
            shape((rows, D), F32),
            shape((rows, 3 * D), BF),
            shape((rows, D), BF),
            shape((rows, heads * CELL), F32),
            shape((rows, D), BF),
            shape((rows, D), F32),
            shape((rows, 128), F32),
            shape((D, 3 * D), BF),
            shape((D, D), BF),
        ],
        [pltpu.VMEM((size, D), BF), pltpu.SemaphoreType.DMA((2 + 16 * (groups - 1),))],
        far=range(6),
        raw=range(6, 6 + count),
    )
    output, keep_up, send_up, resid_back, sums_hidden, bias_sum = run(
        functools.partial(hidden_kernel, ug, groups, len(pieces_up)),
        "hidden",
        place,
        [resid, grad_output, vectors, hidden_bias[None], order, *pieces_up],
        [
            shape(images.shape, BF),
            shape((HALF, 2 * FF), BF),
            shape((HALF, 2 * FF), BF),
            shape((rows, D), F32),
            shape((4, D), F32),
            shape((1, FF), F32),
        ],
        [
            pltpu.VMEM((D, FF), BF),
            pltpu.VMEM((D, FF), BF),
            pltpu.VMEM((size, D), BF),
            pltpu.VMEM((rows, D), BF),
            pltpu.VMEM((rows, D), BF),
            pltpu.VMEM((D, rows), BF),
            pltpu.VMEM((D, rows), BF),
            pltpu.VMEM((rows, D), F32),
            pltpu.VMEM((rows, D), F32),
            pltpu.VMEM((rows, ug), BF),
            pltpu.VMEM((rows, ug), BF),
            pltpu.SemaphoreType.DMA((2 + 16 * (groups - 1),)),
        ],
        far=range(1, 5),
        raw=range(5, 5 + len(pieces_up)),
    )
    keep_proj, send_proj, mixed_back = run(
        proj_kernel,
        "proj",
        place,
        [resid_back, full_proj, mixed],
        [shape((HALF, D), BF), shape((HALF, D), BF), shape((rows, D), BF)],
        [pltpu.VMEM((rows, D), BF), pltpu.VMEM((D, rows), BF)],
    )

    def halve(keep, came, order_by, name):
        width = keep.shape[1]
        return run(
            halve_kernel,
            "halve_" + name,
            after(place, order_by),
            [keep, came],
            [shape((piece, width), F32)] + [shape((piece, width), BF)] * (chips - 1),
            far=(1,),
        )

    def plane(own, sends, order_by, name):
        came = [dshift(item, 2 * (step + 1)) for step, item in enumerate(sends)]
        width = own.shape[1] // groups
        return run(
            functools.partial(plane_kernel, chips),
            "plane_" + name,
            after(place, order_by),
            [own, *came],
            [shape((piece, width), F32)] + [shape((piece, width), BF)] * (groups - 1),
            far=range(1, chips),
        )

    own_up, *sends_up = halve(keep_up, dshift(send_up, 1), mixed_back, "up")
    keep_qkv, send_qkv, qkv_back, sums_scores, table = run(
        functools.partial(scores_kernel, D // heads, groups),
        "scores",
        after(place, own_up),
        [mixed_back, keep_proj, send_proj, qkv_rows, probs, normed, head_mask, ones],
        [
            shape((HALF, 4 * D), BF),
            shape((HALF, 4 * D), BF),
            shape((rows, 3 * D), BF),
            shape((2, D), F32),
            shape((CELL, heads * CELL), F32),
        ],
        [pltpu.VMEM((D, rows), BF)],
        far=(6, 7),
    )
    own_qkv, *sends_qkv = halve(keep_qkv, dshift(send_qkv, 1), table, "qkv")
    input_grad, small = run(
        input_kernel,
        "inputs",
        after(place, own_qkv),
        [
            resid_back,
            qkv_back,
            full_qkv,
            scaled,
            inverse,
            vectors,
            order,
            sums_scores,
            sums_hidden,
            bias_sum,
            table,
            spots,
            bands,
        ],
        [shape(images.shape, F32), shape((12 + heads, D), F32)],
        [pltpu.VMEM((heads * CELL, CELL), F32)],
        far=(5, 6, 11, 12),
    )
    def add(left, right):
        outs = [shape(left.shape, F32)]
        return run(add_kernel, "add", place, [left, right], outs, far=(0, 1))[0]

    own_up, *sends_up = plane(own_up, sends_up, small, "up")
    first = [own_up] + [zshift(item, step + 1) for step, item in enumerate(sends_up)]
    rounds = [functools.partial(dshift, step=1 << bit) for bit in range(members.bit_length() - 1)]
    rounds += [functools.partial(zshift, step=1 << bit) for bit in range(groups.bit_length() - 1)]
    total = after(small, own_qkv)
    for item in rounds[: len(rounds) - 4]:
        total = add(total, item(total))
    own_qkv, *sends_qkv = plane(own_qkv, sends_qkv, total, "qkv")
    second = [own_qkv] + [zshift(item, step + 1) for step, item in enumerate(sends_qkv)]
    total = add(total, rounds[-4](total))
    grad_piece, *outgoing = run(
        functools.partial(momentum_kernel, groups, qg),
        "momentum",
        after(place, total),
        [*first, *second, moment_rows],
        [shape((piece, 2 * ug + qg + pg), BF)] + [shape((piece, ug), BF)] * groups,
        [pltpu.VMEM((max(groups, 4), piece, ug), BF)],
        far=[*range(1, groups), *range(groups + 1, 2 * groups + 1)],
    )

    def share(value):
        near = [value] + [dshift(value, 2 * step) for step in range(1, chips)]
        return near + [dshift(item, 1) for item in near]

    total = add(total, rounds[-3](total))
    owned = [outgoing[0]] + [zshift(outgoing[step], step) for step in range(1, groups)]
    rows_owned = stack(owned, 1, "owned", (total,))
    everyone = share(rows_owned)
    total = add(total, rounds[-2](total))
    results = run(
        functools.partial(newton_kernel, members),
        "newton",
        after(place, total),
        everyone,
        [shape((piece, ug), BF)] * groups,
        [
            pltpu.VMEM((D, groups * ug), BF),
            pltpu.VMEM((D, D), F32),
            pltpu.VMEM((piece, D), F32),
            pltpu.SemaphoreType.DMA((members,)),
        ],
        raw=range(members),
        room=12,
    )
    came = rounds[-1](total)
    back = [results[0]] + [zshift(results[step], step) for step in range(1, groups)]
    states = [
        vectors,
        vector_first,
        vector_second,
        *(item[None] for item in (hidden_bias, bias_first, bias_second)),
        *(item.T for item in (rel_table, table_first, table_second)),
    ]
    adams = run(
        adam_kernel,
        "adam",
        after(place, results[0]),
        [total, came, *states],
        [shape(states[3 * (item // 4)].shape, F32) for item in range(12)],
        far=range(11),
        room=62,
    )
    (packed,) = run(
        functools.partial(pack_kernel, groups, qg),
        "pack",
        after(place, adams[0]),
        back,
        [shape((piece, 2 * ug + qg + pg), BF)],
        [pltpu.VMEM((groups, piece, ug), BF)],
        far=range(groups),
    )
    wide = 2 * ug + qg + pg
    mats = [(D, ug), (ug, D), (D, qg), (D, pg)]
    buffers = [pltpu.VMEM((piece, wide), BF)] * members + [pltpu.VMEM(item, F32) for item in mats]
    double = [item for item in mats for _ in range(2)]
    (
        up_grad,
        up_momentum,
        down_grad,
        down_momentum,
        qkv_grad,
        qkv_momentum,
        proj_grad,
        proj_momentum,
    ) = run(
        functools.partial(grad_kernel, members),
        "grads",
        after(place, packed),
        [*share(after(grad_piece, results[0])), up_moment, down_moment, qkv_moment, proj_moment],
        [shape(item, F32) for item in double],
        [
            *buffers,
            *[pltpu.VMEM(item, F32) for item in mats + mats],
            pltpu.VMEM((D, ug), F32),
            pltpu.SemaphoreType.DMA((members + 4,)),
            pltpu.SemaphoreType.DMA((8,)),
        ],
        raw=range(members + 4),
        sent=range(8),
        room=62,
    )
    new_up, new_down, new_qkv, new_proj = run(
        functools.partial(weight_kernel, members),
        "weights",
        after(place, qkv_grad),
        [*share(packed), up_weight, down_weight, qkv_weight, proj_weight],
        [shape(item, F32) for item in mats],
        [
            *buffers,
            *[pltpu.VMEM(item, F32) for item in mats],
            pltpu.VMEM((D, ug), F32),
            pltpu.SemaphoreType.DMA((members + 4,)),
            pltpu.SemaphoreType.DMA((4,)),
        ],
        raw=range(members + 4),
        sent=range(4),
        room=62,
    )
    vector_grad, new_vectors, vector_mean, vector_square = adams[:4]
    bias_grad, new_bias, bias_mean, bias_square = (item[0] for item in adams[4:8])
    table_grad, new_table, table_mean, table_square = (item.T for item in adams[8:])
    output, input_grad = (after(output, packed), after(input_grad, packed))
    return (
        output,
        input_grad,
        qkv_grad,
        proj_grad,
        up_grad,
        down_grad,
        vector_grad,
        bias_grad,
        table_grad,
        new_qkv,
        new_proj,
        new_up,
        new_down,
        qkv_momentum,
        proj_momentum,
        up_momentum,
        down_momentum,
        new_vectors,
        new_bias,
        new_table,
        vector_mean,
        vector_square,
        bias_mean,
        bias_square,
        table_mean,
        table_square,
    )


def solution(mesh):
    placed = (
        P(("dp", "group"), None, None),
        P(("dp", "group"), None, None),
        P("dp", "group"),
        P(None, "group"),
        P(None, "group"),
        P(None, "group"),
        P("group", None),
        P(None, "group"),
        P(None, "group"),
        P(None, "group"),
        P("group", None),
        P(),
        P(),
        P(),
        P(),
        P(),
        P(),
        P(),
        P(),
        P(),
    )
    return jax.shard_map(
        local,
        mesh=mesh,
        in_specs=placed,
        out_specs=(
            P(("dp", "group"), None, None),
            P(("dp", "group"), None, None),
            P(None, "group"),
            P(None, "group"),
            P(None, "group"),
            P("group", None),
            P(),
            P(),
            P(),
            P(None, "group"),
            P(None, "group"),
            P(None, "group"),
            P("group", None),
            P(None, "group"),
            P(None, "group"),
            P(None, "group"),
            P("group", None),
            P(),
            P(),
            P(),
            P(),
            P(),
            P(),
            P(),
            P(),
            P(),
        ),
        check_vma=False,
    )
```
